128 devices in a mesh: seq: 8 (over x, z_hi), role: 2 (over z_lo), exp: 8 (over y, core).
Axes of the slice: x: 4, y: 4, z: 4 (z_hi: 2, z_lo: 2; z = z_hi * 2 + z_lo), core: 2. Of those that a mesh axis runs over, the one named last changes fastest.
Arguments:
- tokens: bfloat16 [2, 65536, 768], P(None, ('seq', 'role', 'exp')), may hold values from -6 to 6
- expert_ids: int32 [2, 65536, 1], P(None, ('seq', 'role', 'exp')), may hold values from 0 to 127; in each aligned block of 512 rows (0 to 511, 512 to 1023, ..., all dimensions but the last counted through in order) at most 8 rows name the same one
- attn_qkv: bfloat16 [768, 2304], P(('seq', 'role')), may hold values from -0.21875 to 0.21875
- attn_out: bfloat16 [768, 768], P(('seq', 'role')), may hold values from -0.21875 to 0.21875
- norm_attn: float32 [768], replicated, may hold values from 0.1 to 1.9
- norm_ffn: float32 [768], replicated, may hold values from 0.1 to 1.9
- router: bfloat16 [768, 128], replicated, may hold values from -0.43164062 to 0.43164062
- expert_in: bfloat16 [128, 768, 3072], P(('seq', 'role', 'exp')), may hold values from -0.21875 to 0.21875
- expert_out: bfloat16 [128, 3072, 768], P(('seq', 'role', 'exp')), may hold values from -0.109375 to 0.109375
Outputs:
- layer_out: bfloat16 [2, 65536, 768], P(None, ('seq', 'role', 'exp'))
The draws below stay inside these ranges and needn't reach their ends.
Inputs may be any that keep to these rules, and one draw needn't show every extreme that they name: `expert_ids`: in each micro-batch the 512 tokens of one device name any one expert at most 8 times.
All inputs are finite; a program needn't handle non-finite values.
Results may differ from the reference program's by a relative error of at most 0.0058.
Values may be sent and summed in bfloat16 or wider, within the bound.
No kernel may reach another device: no remote copies, remote signals or barrier semaphores. Data moves between devices by JAX's collectives and lax.ppermute only.
A program may use at most 128 MiB of HBM per device.

```python
import math
import jax
import jax.numpy as jnp
import numpy as np
from jax import lax

D = 768
FF = 3072
HEADS = 12
MB = 2
LEN = 512
ROWS = 512
EXPERTS = 128
CAP = 8
TOK_MB = 65536


def shard_levels(own_key, extent, cuts, smallest, top_value):
    def one(axis_at, parts):
        heights = jax.random.uniform(jax.random.fold_in(jax.random.fold_in(own_key, 6), axis_at), (parts,), jnp.float32, smallest / len(cuts), top_value / len(cuts))
        return jnp.repeat(jnp.exp(heights), extent[axis_at] // parts).reshape((-1,) + (1,) * (len(extent) - axis_at - 1))

    gain = one(*cuts[0])
    for cut in cuts[1:]:
        gain = gain * one(*cut)
    return gain


def assign_block(stream_key, own, number, rows, amount, top, most, slope):
    order = jax.random.permutation(stream_key, amount)
    packed, common = portions_of(amount, rows * top, most, slope, True), portions_of(amount, rows * top, most, slope, False)
    places = jnp.arange(amount)

    def named(lengths, offset_by):
        used = int((lengths > 0).sum())
        fixed = max(1, used // 4)
        moved = fixed + (places - fixed + offset_by * (used - fixed)) % max(1, amount - fixed)
        return jnp.zeros((amount,), jnp.int32).at[order[jnp.where(places < fixed, places, moved)]].set(jnp.asarray(lengths, jnp.int32))

    lengths = jnp.where(number % 4 == 0, named(packed, number // 4), named(common, number - number // 4 - 1))
    mixed = jax.random.permutation(jax.random.fold_in(own, 3), amount)
    giver, receiver = mixed[0:amount // 2 * 2:2], mixed[1:amount // 2 * 2:2]
    room = jnp.minimum(lengths[giver] - 1, most - lengths[receiver]) // 2
    room = jnp.where((giver == order[0]) | (receiver == order[0]) | (lengths[receiver] == 0), 0, jnp.maximum(room, 0))
    moved = jax.random.randint(jax.random.fold_in(own, 4), (amount // 2,), 0, 1 << 20) % (room + 1)
    lengths = lengths.at[giver].add(-moved).at[receiver].add(moved)
    labels = jnp.searchsorted(jnp.cumsum(lengths), jnp.arange(rows * top), side="right").astype(jnp.int32)
    table = labels.reshape(top, rows).T
    table = table[jax.random.permutation(jax.random.fold_in(own, 1), rows)]
    offset_by = jax.random.randint(jax.random.fold_in(own, 2), (rows, 1), 0, top)
    return jnp.take_along_axis(table, (jnp.arange(top)[None, :] + offset_by) % top, axis=1)


def portions_of(amount, total, limit, lean, full):
    portions = [(1 << 20) // math.isqrt(grade ** lean) + 1 for grade in range(1, amount + 1)]
    largest = limit if full else min(limit, max(-(-total // amount), total * portions[0] // sum(portions)))
    least = 1 if total - largest >= amount - 1 else 0
    counts, rest = [largest] + [least] * (amount - 1), total - largest - least * (amount - 1)
    while rest > 0:
        free = [i for i in range(1, amount) if counts[i] < largest] or [i for i in range(1, amount) if counts[i] < limit]
        pool, remaining = sum([portions[i] for i in free]), rest
        for i in free:
            more = min(limit - counts[i], max(1, remaining * portions[i] // pool), rest)
            counts[i] = counts[i] + more
            rest = rest - more
    return np.array(counts)


def scatter_about(rng, shape, scale, limit, cuts=(), kind=jnp.bfloat16):
    values = jax.random.normal(rng, shape, jnp.float32) * scale
    if len(cuts) > 0:
        values = shard_levels(rng, shape, cuts, -0.22, 0.18) * values
    return jnp.clip(values, min=-limit, max=limit).astype(kind)


def setup_inputs(seed: int = 0) -> dict:
    key_list = jax.random.split(jax.random.key(seed), 10)
    tokens = scatter_about(key_list[0], (MB, TOK_MB, D), 1.0, 6.0, ((1, 128),))
    expert_ids_keys = jax.random.split(jax.random.fold_in(key_list[1], 1), MB * TOK_MB // ROWS)
    expert_ids_turns = jax.random.permutation(jax.random.fold_in(key_list[1], 3), MB * TOK_MB // ROWS)
    expert_ids = jax.vmap(lambda own, number: assign_block(jax.random.fold_in(key_list[1], 2), own, number, ROWS, EXPERTS, 1, CAP, 2))(expert_ids_keys, expert_ids_turns).reshape((MB, TOK_MB, 1))
    attn_qkv = scatter_about(key_list[2], (D, 3 * D), D ** -0.5, 0.21875, ((0, 16),))
    attn_out = scatter_about(key_list[3], (D, D), D ** -0.5, 0.21875, ((0, 16),))
    norm_attn = jnp.clip(1.0 + 0.18 * jax.random.normal(key_list[4], (D,), jnp.float32), 0.1, 1.9)
    norm_ffn = jnp.clip(1.0 + 0.18 * jax.random.normal(key_list[5], (D,), jnp.float32), 0.1, 1.9)
    router = scatter_about(key_list[6], (D, EXPERTS), (2.0 / D ** 0.5), 0.43164062)
    expert_in = scatter_about(key_list[7], (EXPERTS, D, FF), D ** -0.5, 0.21875, ((0, 128),))
    expert_out = scatter_about(key_list[8], (EXPERTS, FF, D), FF ** -0.5, 0.109375, ((0, 128),))
    return dict(tokens=tokens, expert_ids=expert_ids, attn_qkv=attn_qkv, attn_out=attn_out, norm_attn=norm_attn, norm_ffn=norm_ffn, router=router, expert_in=expert_in, expert_out=expert_out)


def scale_rows(values, gain_vec):
    floats = values.astype(jnp.float32)
    return floats * lax.rsqrt(lax.optimization_barrier(jnp.mean(floats * floats, -1, keepdims=True)) + 1e-06) * gain_vec.astype(jnp.float32)

def reference(tokens, expert_ids, attn_qkv, attn_out, norm_attn, norm_ffn, router, expert_in, expert_out):
    token_total = MB * TOK_MB
    head_dim = D // HEADS
    flat_tokens = tokens.reshape(token_total, D)
    normed = scale_rows(flat_tokens, norm_attn).astype(jnp.bfloat16)

    def attend(sequence):
        projected = jnp.dot(sequence, attn_qkv, preferred_element_type=jnp.float32).astype(jnp.bfloat16)
        projected = lax.optimization_barrier(projected)
        heads_split = projected.reshape(LEN, 3, HEADS, head_dim).astype(jnp.float32)
        scores = jnp.einsum('qhd,khd->hqk', heads_split[:, 0], heads_split[:, 1]) * head_dim ** (-0.5)
        weights = jnp.exp(scores)
        weights_norm = (weights / lax.optimization_barrier(jnp.sum(weights, -1, keepdims=True))).astype(jnp.bfloat16)
        weights_norm = lax.optimization_barrier(weights_norm).astype(jnp.float32)
        context = jnp.einsum('hqk,khd->qhd', weights_norm, heads_split[:, 2]).astype(jnp.bfloat16)
        return context.reshape(LEN, D)
    context = lax.map(attend, normed.reshape(token_total // LEN, LEN, D)).reshape(token_total, D)
    attended = (flat_tokens.astype(jnp.float32) + jnp.dot(context, attn_out, preferred_element_type=jnp.float32)).astype(jnp.bfloat16)
    normed_ffn = scale_rows(attended, norm_ffn).astype(jnp.bfloat16)
    chosen_ids = expert_ids.reshape(token_total).astype(jnp.int32)
    logits = jnp.dot(normed_ffn, router, preferred_element_type=jnp.float32)
    chosen = jnp.take_along_axis(logits, chosen_ids[:, None], axis=1)[:, 0]
    gate_value = jax.nn.sigmoid(chosen)
    block_count = token_total // ROWS
    grouped = chosen_ids.reshape(block_count, ROWS)
    onehot = (grouped[:, :, None] == jnp.arange(EXPERTS, dtype=jnp.int32)[None, None, :]).astype(jnp.int32)
    slot_index = lax.optimization_barrier(jnp.sum(onehot * jnp.cumsum(onehot, axis=1), -1)) - 1
    block_index = jnp.arange(block_count, dtype=jnp.int32)[:, None]
    position = (grouped * (block_count * CAP) + block_index * CAP + slot_index).reshape(token_total).astype(jnp.int32)
    buffer = jnp.zeros((EXPERTS * block_count * CAP, D), jnp.bfloat16).at[position].set(normed_ffn)

    def serve_rows(expert_pair):
        rows_in, weight_in, weight_out = expert_pair
        hidden = jax.nn.relu(jnp.dot(rows_in, weight_in, preferred_element_type=jnp.float32)).astype(jnp.bfloat16)
        return jnp.dot(hidden, weight_out, preferred_element_type=jnp.float32).astype(jnp.bfloat16)
    served = lax.map(serve_rows, (buffer.reshape(EXPERTS, block_count * CAP, D), expert_in, expert_out))
    result = served.reshape(EXPERTS * block_count * CAP, D)[position]
    layer_out = (attended.astype(jnp.float32) + gate_value[:, None] * result.astype(jnp.float32)).astype(jnp.bfloat16)
    return layer_out.reshape(MB, TOK_MB, D)
```

```python
import functools

import jax
import jax.numpy as jnp
from jax import lax
from jax.experimental import pallas as pl
from jax.experimental.pallas import tpu as pltpu
from jax.sharding import PartitionSpec as P

HEADS = 12
HALF = 384
SLOTS = 8
ALL = ("seq", "role", "exp")
F32 = jnp.float32
BF16 = jnp.bfloat16


def place(x, z, y, c):
    return x * 32 + z * 8 + y * 2 + c


def hop(d, phase):
    pairs = []
    for x in range(4):
        for z in range(4):
            for y in range(4):
                for c in range(2):
                    if (c == 0) == (phase == 0):
                        to = place((x + d) % 4, z, y, c)
                    else:
                        to = place(x, (z + d) % 4, y, c)
                    pairs.append((place(x, z, y, c), to))
    return pairs


def my_core():
    return lax.rem(lax.axis_index("exp"), 2)


def scale_rows(values, gain):
    floats = values.astype(F32)
    return floats * lax.rsqrt(jnp.mean(floats * floats, -1, keepdims=True) + 1e-06) * gain


def assemble_kernel(b0, b1, b2, b3, w_ref, sem):
    seq = lax.axis_index("seq")
    x = seq // 2
    z = lax.rem(seq, 2) * 2 + lax.axis_index("role")
    core = my_core()
    shift = (0, 3, 1, 2)
    copies = []
    for i, block in enumerate((b0, b1, b2, b3)):
        for j in range(4):
            dx = jnp.where(core == 0, shift[j], shift[i])
            dz = jnp.where(core == 0, shift[i], shift[j])
            row = (lax.rem(x + dx, 4) * 4 + lax.rem(z + dz, 4)) * 48
            copies.append(
                pltpu.make_async_copy(
                    block.at[pl.ds(j * 48, 48), :],
                    w_ref.at[pl.ds(pl.multiple_of(row, 16), 48), :],
                    sem.at[i * 4 + j],
                )
            )
    for copy in copies:
        copy.start()
    for copy in copies:
        copy.wait()


def assemble(blocks):
    any_spec = pl.BlockSpec(memory_space=pl.ANY)
    return pl.pallas_call(
        assemble_kernel,
        out_shape=jax.ShapeDtypeStruct((768, blocks[0].shape[1]), BF16),
        in_specs=[any_spec] * 4,
        out_specs=any_spec,
        scratch_shapes=[pltpu.SemaphoreType.DMA((16,))],
        name="assemble",
    )(*blocks)


def half_context(normed, weights):
    rows = normed.shape[0]
    projected = jnp.dot(normed, weights, preferred_element_type=F32).astype(BF16)
    low = lax.broadcasted_iota(jnp.int32, (rows, 128), 1) < 64
    ones = jnp.ones((rows, 128), BF16)
    zero = jnp.zeros((rows, 128), BF16)
    pieces = []
    for pair in range(3):
        q = projected[:, pair * 128 : pair * 128 + 128] * jnp.asarray(0.125, BF16)
        k = projected[:, HALF + pair * 128 : HALF + pair * 128 + 128]
        v = projected[:, 2 * HALF + pair * 128 : 2 * HALF + pair * 128 + 128]
        values = jnp.concatenate([v, ones], axis=1)
        outs = []
        for side in range(2):
            mine = jnp.where(low, q, zero) if side == 0 else jnp.where(low, zero, q)
            scores = lax.dot_general(
                mine, k, (((1,), (1,)), ((), ())), preferred_element_type=F32
            )
            top = jnp.max(scores, -1, keepdims=True)
            weight = jnp.exp(scores - top).astype(BF16)
            total = jnp.dot(weight, values, preferred_element_type=F32)
            outs.append(total[:, :128] / total[:, 128:])
        pieces.append(jnp.where(low, outs[0], outs[1]).astype(BF16))
    return jnp.concatenate(pieces, axis=1)


def context_kernel(x_ref, gain_ref, w_ref, ctx_ref):
    normed = scale_rows(x_ref[0], gain_ref[...]).astype(BF16)
    ctx_ref[...] = half_context(normed, w_ref[:, : 3 * HALF])


def finish(x, ctx, w, gain, router, ids_row, ids_col, att_ref, out_ref, aux_ref):
    rows = x.shape[0]
    mixed = []
    for side in range(2):
        columns = w[side, :, 3 * HALF :]
        mixed.append(
            jnp.dot(ctx[0], columns[:HALF], preferred_element_type=F32)
            + jnp.dot(ctx[1], columns[HALF:], preferred_element_type=F32)
        )
    attended = (x.astype(F32) + jnp.concatenate(mixed, axis=1)).astype(BF16)
    att_ref[...] = attended
    normed = scale_rows(attended, gain).astype(BF16)
    experts = router.shape[1]
    logits = jnp.dot(normed, router, preferred_element_type=F32)
    i0 = lax.broadcasted_iota(jnp.int32, (rows, rows), 0)
    i1 = lax.broadcasted_iota(jnp.int32, (rows, rows), 1)
    picked = ids_col == lax.broadcasted_iota(jnp.int32, (rows, experts), 1)
    gate = jax.nn.sigmoid(jnp.sum(jnp.where(picked, logits, 0.0), -1, keepdims=True))
    running = jnp.dot(
        (i0 >= i1).astype(F32).astype(BF16),
        picked.astype(F32).astype(BF16),
        preferred_element_type=F32,
    )
    rank = jnp.sum(jnp.where(picked, running, 0.0), -1, keepdims=True)
    position = ids_col.astype(F32) * SLOTS + rank - 1.0
    aux_lane = lax.broadcasted_iota(jnp.int32, (rows, 128), 1)
    aux_ref[...] = jnp.where(aux_lane == 0, gate, position)
    picked_t = ids_row == lax.broadcasted_iota(jnp.int32, (experts, rows), 0)
    running_t = jnp.dot(
        picked_t.astype(F32).astype(BF16),
        (i0 <= i1).astype(F32).astype(BF16),
        preferred_element_type=F32,
    )
    rank_t = jnp.sum(jnp.where(picked_t, running_t, 0.0), 0, keepdims=True)
    position_t = ids_row * SLOTS + rank_t.astype(jnp.int32) - 1
    slots = experts * SLOTS
    spread = (lax.broadcasted_iota(jnp.int32, (slots, rows), 0) == position_t).astype(F32).astype(BF16)
    out_ref[...] = jnp.dot(spread, normed, preferred_element_type=F32).astype(BF16)


def load_weights(mine_ref, other_ref, w, sems):
    core = my_core()
    first = pltpu.make_async_copy(mine_ref, w.at[core], sems.at[0])
    second = pltpu.make_async_copy(other_ref, w.at[1 - core], sems.at[1])
    first.start()
    second.start()
    first.wait()
    second.wait()
    return core


def second_half_kernel(
    x_ref, gain_ref, mine_ref, other_ref, ctx_ref, gain2_ref, router_ref, row_ref, col_ref,
    att_ref, out_ref, aux_ref, w, ctx, sems,
):
    core = load_weights(mine_ref, other_ref, w, sems)
    normed = scale_rows(x_ref[0], gain_ref[...]).astype(BF16)
    ctx[core] = ctx_ref[...]
    ctx[1 - core] = half_context(normed, w[1 - core, :, : 3 * HALF])
    finish(
        x_ref[0], ctx, w, gain2_ref[...], router_ref[...], row_ref[0], col_ref[0],
        att_ref, out_ref, aux_ref,
    )


def whole_kernel(
    x_ref, gain_ref, mine_ref, other_ref, gain2_ref, router_ref, row_ref, col_ref,
    att_ref, out_ref, aux_ref, w, ctx, sems,
):
    load_weights(mine_ref, other_ref, w, sems)
    normed = scale_rows(x_ref[0], gain_ref[...]).astype(BF16)

    def step(side, carry):
        ctx[side] = half_context(normed, w[side, :, : 3 * HALF])
        return carry

    lax.fori_loop(0, 2, step, 0)
    finish(
        x_ref[0], ctx, w, gain2_ref[...], router_ref[...], row_ref[0], col_ref[0],
        att_ref, out_ref, aux_ref,
    )


def combine_kernel(att_ref, aux_ref, back_ref, out_ref):
    rows, slots = att_ref.shape[0], back_ref.shape[0]
    gate = aux_ref[:, 0:1]
    position = aux_ref[:, 1:2].astype(jnp.int32)
    pick = (lax.broadcasted_iota(jnp.int32, (rows, slots), 1) == position).astype(F32).astype(BF16)
    result = jnp.dot(pick, back_ref[...], preferred_element_type=F32)
    out_ref[0] = (att_ref[...].astype(F32) + gate * result).astype(BF16)


def combine_after_kernel(att_ref, aux_ref, back_ref, held_ref, out_ref):
    del held_ref
    combine_kernel(att_ref, aux_ref, back_ref, out_ref)


def full(shape):
    return pl.BlockSpec(shape, lambda i: (0,) * len(shape))


def body(
    tokens, expert_ids, attn_qkv, attn_out, norm_attn, norm_ffn, router, expert_in, expert_out
):
    batches, rows, width = tokens.shape
    experts = router.shape[1]
    slots = experts * SLOTS
    core = my_core()
    parts = attn_qkv.reshape(48, 3, 2, HALF)
    out_parts = attn_out.reshape(48, 1, 2, HALF)
    parts = jnp.concatenate([parts, out_parts], axis=1)
    piece = jnp.where(core == 0, parts[:, :, 0], parts[:, :, 1]).reshape(48, 4 * HALF)
    block = jnp.concatenate(
        [piece] + [lax.ppermute(piece, ALL, hop(d, 0)) for d in (1, -1, 2)], axis=0
    )
    others = [lax.ppermute(block, ALL, hop(d, 1)) for d in (1, -1, 2)]
    w_mine = assemble([block] + others)
    w_other = lax.ppermute(w_mine, ALL, [(i, i ^ 1) for i in range(128)])

    gain = norm_attn.reshape(1, width)
    gain2 = norm_ffn.reshape(1, width)
    ids_row = expert_ids.reshape(batches, 1, rows)

    def token_spec(b):
        return pl.BlockSpec((1, rows, width), lambda i: (b, 0, 0))

    any_spec = pl.BlockSpec(memory_space=pl.ANY)
    ctx_mine = pl.pallas_call(
        context_kernel,
        grid=(1,),
        out_shape=jax.ShapeDtypeStruct((rows, HALF), BF16),
        in_specs=[token_spec(0), full((1, width)), full((width, 4 * HALF))],
        out_specs=full((rows, HALF)),
        name="first_half",
    )(tokens, gain, w_mine)

    finish_out = (
        jax.ShapeDtypeStruct((rows, width), BF16),
        jax.ShapeDtypeStruct((slots, width), BF16),
        jax.ShapeDtypeStruct((rows, 128), F32),
    )
    finish_specs = (full((rows, width)), full((slots, width)), full((rows, 128)))
    scratch = [
        pltpu.VMEM((2, width, 4 * HALF), BF16),
        pltpu.VMEM((2, rows, HALF), BF16),
        pltpu.SemaphoreType.DMA((2,)),
    ]

    def tail_specs(b):
        return [
            full((1, width)),
            full((width, experts)),
            pl.BlockSpec((1, 1, rows), lambda i: (b, 0, 0)),
            pl.BlockSpec((1, rows, 1), lambda i: (b, 0, 0)),
        ]

    first = pl.pallas_call(
        second_half_kernel,
        grid=(1,),
        out_shape=finish_out,
        in_specs=[token_spec(0), full((1, width)), any_spec, any_spec, full((rows, HALF))]
        + tail_specs(0),
        out_specs=finish_specs,
        scratch_shapes=scratch,
        name="second_half",
    )(tokens, gain, w_mine, w_other, ctx_mine, gain2, router, ids_row, expert_ids)

    second = pl.pallas_call(
        whole_kernel,
        grid=(1,),
        out_shape=finish_out,
        in_specs=[token_spec(1), full((1, width)), any_spec, any_spec] + tail_specs(1),
        out_specs=finish_specs,
        scratch_shapes=scratch,
        name="whole",
    )(tokens, gain, w_mine, w_other, gain2, router, ids_row, expert_ids)

    weight_in = expert_in[0]
    weight_out = expert_out[0]

    def exchange(values):
        return lax.all_to_all(
            values.reshape(experts, SLOTS, width), ALL, split_axis=0, concat_axis=0, tiled=True
        ).reshape(slots, width)

    def serve(values):
        hidden = jax.nn.relu(jnp.dot(values, weight_in, preferred_element_type=F32)).astype(BF16)
        return jnp.dot(hidden, weight_out, preferred_element_type=F32).astype(BF16)

    arrived = [exchange(first[1]), exchange(second[1])]
    back = [exchange(serve(values)) for values in arrived]

    out_shape = jax.ShapeDtypeStruct((batches, rows, width), BF16)
    specs = [full((rows, width)), full((rows, 128)), full((slots, width))]
    held = pl.pallas_call(
        combine_kernel,
        grid=(1,),
        out_shape=out_shape,
        in_specs=specs,
        out_specs=token_spec(0),
        name="combine0",
    )(first[0], first[2], back[0])
    return pl.pallas_call(
        combine_after_kernel,
        grid=(1,),
        out_shape=out_shape,
        in_specs=specs + [any_spec],
        out_specs=token_spec(1),
        input_output_aliases={3: 0},
        name="combine1",
    )(second[0], second[2], back[1], held)


def solution(mesh):
    in_specs = (
        P(None, ALL, None),
        P(None, ALL, None),
        P(("seq", "role"), None),
        P(("seq", "role"), None),
        P(),
        P(),
        P(),
        P(ALL, None, None),
        P(ALL, None, None),
    )
    return jax.shard_map(
        body, mesh=mesh, in_specs=in_specs, out_specs=P(None, ALL, None), check_vma=False
    )
```

```python
import functools

import jax
import jax.numpy as jnp
from jax import lax
from jax.experimental import pallas as pl
from jax.experimental.pallas import tpu as pltpu
from jax.sharding import PartitionSpec as P

HEADS = 12
HALF = 384
SLOTS = 8
ALL = ("seq", "role", "exp")
F32 = jnp.float32
BF16 = jnp.bfloat16


def place(x, z, y, c):
    return x * 32 + z * 8 + y * 2 + c


def hop(d, phase):
    pairs = []
    for x in range(4):
        for z in range(4):
            for y in range(4):
                for c in range(2):
                    if (c == 0) == (phase == 0):
                        to = place((x + d) % 4, z, y, c)
                    else:
                        to = place(x, (z + d) % 4, y, c)
                    pairs.append((place(x, z, y, c), to))
    return pairs


def my_core():
    return lax.rem(lax.axis_index("exp"), 2)


def scale_rows(values, gain):
    floats = values.astype(F32)
    return floats * lax.rsqrt(jnp.mean(floats * floats, -1, keepdims=True) + 1e-06) * gain


def fetch(blocks, core, w, sem):
    seq = lax.axis_index("seq")
    x = seq // 2
    z = lax.rem(seq, 2) * 2 + lax.axis_index("role")
    shift = (0, 3, 1, 2)
    copies = []
    for i, block in enumerate(blocks):
        for j in range(4):
            dx = jnp.where(core == 0, shift[j], shift[i])
            dz = jnp.where(core == 0, shift[i], shift[j])
            row = (lax.rem(x + dx, 4) * 4 + lax.rem(z + dz, 4)) * 48
            copies.append(
                pltpu.make_async_copy(
                    block.at[pl.ds(j * 48, 48), :],
                    w.at[core, pl.ds(pl.multiple_of(row, 16), 48), :],
                    sem.at[i * 4 + j],
                )
            )
    for copy in copies:
        copy.start()
    return copies


def wait_all(copies):
    for copy in copies:
        copy.wait()


def half_context(normed, weights):
    rows = normed.shape[0]
    projected = jnp.dot(normed, weights, preferred_element_type=F32).astype(BF16)
    low = lax.broadcasted_iota(jnp.int32, (rows, 128), 1) < 64
    ones = jnp.ones((rows, 128), BF16)
    zero = jnp.zeros((rows, 128), BF16)
    pieces = []
    for pair in range(3):
        q = projected[:, pair * 128 : pair * 128 + 128] * jnp.asarray(0.125, BF16)
        k = projected[:, HALF + pair * 128 : HALF + pair * 128 + 128]
        v = projected[:, 2 * HALF + pair * 128 : 2 * HALF + pair * 128 + 128]
        values = jnp.concatenate([v, ones], axis=1)
        outs = []
        for side in range(2):
            mine = jnp.where(low, q, zero) if side == 0 else jnp.where(low, zero, q)
            scores = lax.dot_general(
                mine, k, (((1,), (1,)), ((), ())), preferred_element_type=F32
            )
            top = jnp.max(scores, -1, keepdims=True)
            weight = jnp.exp(scores - top).astype(BF16)
            total = jnp.dot(weight, values, preferred_element_type=F32)
            outs.append(total[:, :128] / total[:, 128:])
        pieces.append(jnp.where(low, outs[0], outs[1]).astype(BF16))
    return jnp.concatenate(pieces, axis=1)


def context_kernel(x_ref, gain_ref, b0, b1, b2, b3, ctx_ref, w, sem):
    core = my_core()
    copies = fetch((b0, b1, b2, b3), core, w, sem)
    normed = scale_rows(x_ref[0], gain_ref[...]).astype(BF16)
    wait_all(copies)
    ctx_ref[...] = half_context(normed, w[core, :, : 3 * HALF])


def finish(x, ctx, w, gain, router, ids_row, att_ref, out_ref, aux_ref):
    rows = x.shape[0]
    mixed = []
    for side in range(2):
        columns = w[side, :, 3 * HALF :]
        mixed.append(
            jnp.dot(ctx[0], columns[:HALF], preferred_element_type=F32)
            + jnp.dot(ctx[1], columns[HALF:], preferred_element_type=F32)
        )
    attended = (x.astype(F32) + jnp.concatenate(mixed, axis=1)).astype(BF16)
    att_ref[...] = attended
    normed = scale_rows(attended, gain).astype(BF16)
    experts = router.shape[1]
    logits = lax.dot_general(
        router, normed, (((0,), (1,)), ((), ())), preferred_element_type=F32
    )
    i0 = lax.broadcasted_iota(jnp.int32, (rows, rows), 0)
    i1 = lax.broadcasted_iota(jnp.int32, (rows, rows), 1)
    picked = ids_row == lax.broadcasted_iota(jnp.int32, (experts, rows), 0)
    gate = jax.nn.sigmoid(jnp.sum(jnp.where(picked, logits, 0.0), 0, keepdims=True))
    running = jnp.dot(
        picked.astype(F32).astype(BF16),
        (i0 <= i1).astype(F32).astype(BF16),
        preferred_element_type=F32,
    )
    rank = jnp.sum(jnp.where(picked, running, 0.0), 0, keepdims=True)
    position = ids_row * SLOTS + rank.astype(jnp.int32) - 1
    aux_row = lax.broadcasted_iota(jnp.int32, (128, rows), 0)
    aux_ref[...] = jnp.where(aux_row == 0, gate, position.astype(F32)).T
    slots = experts * SLOTS
    spread = (lax.broadcasted_iota(jnp.int32, (slots, rows), 0) == position).astype(F32).astype(BF16)
    out_ref[...] = jnp.dot(spread, normed, preferred_element_type=F32).astype(BF16)


def second_half_kernel(
    x_ref, gain_ref, m0, m1, m2, m3, o0, o1, o2, o3, ctx_ref, gain2_ref, router_ref, row_ref,
    att_ref, out_ref, aux_ref, w, ctx, sems,
):
    core = my_core()
    other = fetch((o0, o1, o2, o3), 1 - core, w, sems.at[1])
    mine = fetch((m0, m1, m2, m3), core, w, sems.at[0])
    normed = scale_rows(x_ref[0], gain_ref[...]).astype(BF16)
    ctx[core] = ctx_ref[...]
    wait_all(other)
    ctx[1 - core] = half_context(normed, w[1 - core, :, : 3 * HALF])
    wait_all(mine)
    finish(
        x_ref[0], ctx, w, gain2_ref[...], router_ref[...], row_ref[0],
        att_ref, out_ref, aux_ref,
    )


def whole_kernel(
    x_ref, gain_ref, m0, m1, m2, m3, o0, o1, o2, o3, gain2_ref, router_ref, row_ref,
    att_ref, out_ref, aux_ref, w, ctx, sems,
):
    core = my_core()
    copies = fetch((m0, m1, m2, m3), core, w, sems.at[0])
    copies = copies + fetch((o0, o1, o2, o3), 1 - core, w, sems.at[1])
    normed = scale_rows(x_ref[0], gain_ref[...]).astype(BF16)
    wait_all(copies)

    def step(side, carry):
        ctx[side] = half_context(normed, w[side, :, : 3 * HALF])
        return carry

    lax.fori_loop(0, 2, step, 0)
    finish(
        x_ref[0], ctx, w, gain2_ref[...], router_ref[...], row_ref[0],
        att_ref, out_ref, aux_ref,
    )


def combine_kernel(att_ref, aux_ref, back_ref, out_ref):
    rows, slots = att_ref.shape[0], back_ref.shape[0]
    gate = aux_ref[:, 0:1]
    position = aux_ref[:, 1:2].astype(jnp.int32)
    pick = (lax.broadcasted_iota(jnp.int32, (rows, slots), 1) == position).astype(F32).astype(BF16)
    result = jnp.dot(pick, back_ref[...], preferred_element_type=F32)
    out_ref[0] = (att_ref[...].astype(F32) + gate * result).astype(BF16)


def combine_after_kernel(att_ref, aux_ref, back_ref, held_ref, out_ref):
    del held_ref
    combine_kernel(att_ref, aux_ref, back_ref, out_ref)


def full(shape):
    return pl.BlockSpec(shape, lambda i: (0,) * len(shape))


def body(
    tokens, expert_ids, attn_qkv, attn_out, norm_attn, norm_ffn, router, expert_in, expert_out
):
    batches, rows, width = tokens.shape
    experts = router.shape[1]
    slots = experts * SLOTS
    core = my_core()
    halves = [
        jnp.concatenate(
            [attn_qkv[:, at + side * HALF : at + side * HALF + HALF] for at in (0, width, 2 * width)]
            + [attn_out[:, side * HALF : side * HALF + HALF]],
            axis=1,
        )
        for side in range(2)
    ]
    piece = jnp.where(core == 0, halves[0], halves[1])
    swap = [(i, i ^ 1) for i in range(128)]
    block = jnp.concatenate(
        [piece] + [lax.ppermute(piece, ALL, hop(d, 0)) for d in (1, -1, 2)], axis=0
    )
    mine = [block] + [lax.ppermute(block, ALL, hop(d, 1)) for d in (1, -1, 2)]
    other = [lax.ppermute(part, ALL, swap) for part in mine]

    ids_row = expert_ids.reshape(batches, 1, rows)

    def token_spec(b):
        return pl.BlockSpec((1, rows, width), lambda i: (b, 0, 0))

    any_spec = pl.BlockSpec(memory_space=pl.ANY)
    w_scratch = pltpu.VMEM((2, width, 4 * HALF), BF16)
    ctx_mine = pl.pallas_call(
        context_kernel,
        grid=(1,),
        out_shape=jax.ShapeDtypeStruct((rows, HALF), BF16),
        in_specs=[token_spec(0), full((width,))] + [any_spec] * 4,
        out_specs=full((rows, HALF)),
        scratch_shapes=[w_scratch, pltpu.SemaphoreType.DMA((16,))],
        name="first_half",
    )(tokens, norm_attn, *mine)

    finish_out = (
        jax.ShapeDtypeStruct((rows, width), BF16),
        jax.ShapeDtypeStruct((slots, width), BF16),
        jax.ShapeDtypeStruct((rows, 128), F32),
    )
    finish_specs = (full((rows, width)), full((slots, width)), full((rows, 128)))
    scratch = [
        w_scratch,
        pltpu.VMEM((2, rows, HALF), BF16),
        pltpu.SemaphoreType.DMA((2, 16)),
    ]

    def tail_specs(b):
        return [
            full((width,)),
            full((width, experts)),
            pl.BlockSpec((1, 1, rows), lambda i: (b, 0, 0)),
        ]

    first = pl.pallas_call(
        second_half_kernel,
        grid=(1,),
        out_shape=finish_out,
        in_specs=[token_spec(0), full((width,))] + [any_spec] * 8 + [full((rows, HALF))]
        + tail_specs(0),
        out_specs=finish_specs,
        scratch_shapes=scratch,
        name="second_half",
    )(tokens, norm_attn, *mine, *other, ctx_mine, norm_ffn, router, ids_row)

    second = pl.pallas_call(
        whole_kernel,
        grid=(1,),
        out_shape=finish_out,
        in_specs=[token_spec(1), full((width,))] + [any_spec] * 8 + tail_specs(1),
        out_specs=finish_specs,
        scratch_shapes=scratch,
        name="whole",
    )(tokens, norm_attn, *mine, *other, norm_ffn, router, ids_row)

    weight_in = expert_in[0]
    weight_out = expert_out[0]

    def exchange(values):
        return lax.all_to_all(
            values.reshape(experts, SLOTS, width), ALL, split_axis=0, concat_axis=0, tiled=True
        ).reshape(slots, width)

    def serve(values):
        hidden = jax.nn.relu(jnp.dot(values, weight_in, preferred_element_type=F32)).astype(BF16)
        return jnp.dot(hidden, weight_out, preferred_element_type=F32).astype(BF16)

    arrived = [exchange(first[1]), exchange(second[1])]
    back = [exchange(serve(values)) for values in arrived]

    out_shape = jax.ShapeDtypeStruct((batches, rows, width), BF16)
    specs = [full((rows, width)), full((rows, 128)), full((slots, width))]
    held = pl.pallas_call(
        combine_kernel,
        grid=(1,),
        out_shape=out_shape,
        in_specs=specs,
        out_specs=token_spec(0),
        name="combine0",
    )(first[0], first[2], back[0])
    return pl.pallas_call(
        combine_after_kernel,
        grid=(1,),
        out_shape=out_shape,
        in_specs=specs + [any_spec],
        out_specs=token_spec(1),
        input_output_aliases={3: 0},
        name="combine1",
    )(second[0], second[2], back[1], held)


def solution(mesh):
    in_specs = (
        P(None, ALL, None),
        P(None, ALL, None),
        P(("seq", "role"), None),
        P(("seq", "role"), None),
        P(),
        P(),
        P(),
        P(ALL, None, None),
        P(ALL, None, None),
    )
    return jax.shard_map(
        body, mesh=mesh, in_specs=in_specs, out_specs=P(None, ALL, None), check_vma=False
    )
```

```python
import functools

import jax
import jax.numpy as jnp
from jax import lax
from jax.experimental import pallas as pl
from jax.experimental.pallas import tpu as pltpu
from jax.sharding import PartitionSpec as P

HEADS = 12
HALF = 384
SLOTS = 8
ALL = ("seq", "role", "exp")
F32 = jnp.float32
BF16 = jnp.bfloat16


def place(x, z, y, c):
    return x * 32 + z * 8 + y * 2 + c


def hop(d, phase):
    pairs = []
    for x in range(4):
        for z in range(4):
            for y in range(4):
                for c in range(2):
                    if (c == 0) == (phase == 0):
                        to = place((x + d) % 4, z, y, c)
                    else:
                        to = place(x, (z + d) % 4, y, c)
                    pairs.append((place(x, z, y, c), to))
    return pairs


def my_core():
    return lax.rem(lax.axis_index("exp"), 2)


def scale_rows(values, gain):
    floats = values.astype(F32)
    return floats * lax.rsqrt(jnp.mean(floats * floats, -1, keepdims=True) + 1e-06) * gain


def fetch(blocks, core, w, sem, wo=None, wo_sem=None):
    own, rest = blocks
    seq = lax.axis_index("seq")
    x = seq // 2
    z = lax.rem(seq, 2) * 2 + lax.axis_index("role")
    shift = (0, 3, 1, 2)
    copies, late = [], []
    for i in range(4):
        for j in range(4):
            source, at = (own, j * 48) if i == 0 else (rest, (i * 4 + j - 4) * 48)
            dx = jnp.where(core == 0, shift[j], shift[i])
            dz = jnp.where(core == 0, shift[i], shift[j])
            row = (lax.rem(x + dx, 4) * 4 + lax.rem(z + dz, 4)) * 48
            row = pl.multiple_of(row, 16)
            if w is not None:
                copies.append(
                    pltpu.make_async_copy(
                        source.at[pl.ds(at, 48), pl.ds(0, 3 * HALF)],
                        w.at[core, pl.ds(row, 48), :],
                        sem.at[i * 4 + j],
                    )
                )
            if wo is not None:
                late.append(
                    pltpu.make_async_copy(
                        source.at[pl.ds(at, 48), pl.ds(3 * HALF, HALF)],
                        wo.at[pl.ds(row, 48), pl.ds(pl.multiple_of(core * HALF, 128), HALF)],
                        wo_sem.at[i * 4 + j],
                    )
                )
    for copy in copies + late:
        copy.start()
    return copies, late


def wait_all(copies):
    for copy in copies:
        copy.wait()


def project(normed, weights, projected):
    projected[...] = jnp.dot(normed[...], weights[...], preferred_element_type=F32).astype(BF16)


def start_all(pairs, sems):
    copies = [
        pltpu.make_async_copy(source, target, sems.at[i]) for i, (source, target) in enumerate(pairs)
    ]
    for copy in copies:
        copy.start()
    return copies


def attend(projected, store):
    rows = projected.shape[0]
    block = 256
    low = lax.broadcasted_iota(jnp.int32, (block, 128), 1) < 64
    for pair in range(3):
        at = pair * 128
        k = projected[:, HALF + at : HALF + at + 128]
        v = projected[:, 2 * HALF + at : 2 * HALF + at + 128]
        values = jnp.concatenate([v, jnp.ones((rows, 128), BF16)], axis=1)
        for row in range(0, rows, block):
            q = projected[row : row + block, at : at + 128] * jnp.asarray(0.125, BF16)
            zero = jnp.zeros_like(q)
            outs = []
            for side in range(2):
                mine = jnp.where(low, q, zero) if side == 0 else jnp.where(low, zero, q)
                scores = lax.dot_general(
                    mine, k, (((1,), (1,)), ((), ())), preferred_element_type=F32
                )
                weight = jnp.exp(scores - jnp.max(scores, -1, keepdims=True)).astype(BF16)
                total = jnp.dot(weight, values, preferred_element_type=F32)
                outs.append(total[:, :128] / total[:, 128:])
            store(pair, row, jnp.where(low, outs[0], outs[1]).astype(BF16))


def context_kernel(
    x_ref, gain_ref, b0, b1, ctx_ref, normed_ref, x, gain, w, projected, sem, small
):
    core = my_core()
    loads = start_all([(x_ref.at[0], x), (gain_ref, gain)], small)
    copies, _ = fetch((b0, b1), core, w, sem)
    wait_all(loads)
    normed_ref[...] = scale_rows(x[...], gain[...]).astype(BF16)
    wait_all(copies)
    project(normed_ref, w.at[core], projected)

    def store(pair, row, context):
        ctx_ref[row : row + context.shape[0], pair * 128 : pair * 128 + 128] = context

    attend(projected, store)


def finish(
    x, ctx, wo, gain, router, ids, att_ref, out_ref, aux_ref, normed, sent, att, aux, sems
):
    rows, experts = x.shape[0], router.shape[1]
    block = 256
    for row in range(0, rows, block):
        mine = slice(row, row + block)
        both = jnp.concatenate([ctx[0, mine], ctx[1, mine]], axis=1)
        mixed = jnp.dot(both, wo[...], preferred_element_type=F32)
        attended = (x[mine].astype(F32) + mixed).astype(BF16)
        att[mine] = attended
        normed[mine] = scale_rows(attended, gain[...]).astype(BF16)
    copies = [pltpu.make_async_copy(att, att_ref, sems.at[4])]
    copies[0].start()
    ids_row = ids[...]
    logits = lax.dot_general(
        router[...], normed[...], (((0,), (1,)), ((), ())), preferred_element_type=F32
    )
    i0 = lax.broadcasted_iota(jnp.int32, (rows, rows), 0)
    i1 = lax.broadcasted_iota(jnp.int32, (rows, rows), 1)
    picked = ids_row == lax.broadcasted_iota(jnp.int32, (experts, rows), 0)
    gate = jax.nn.sigmoid(jnp.sum(jnp.where(picked, logits, 0.0), 0, keepdims=True))
    running = jnp.dot(
        picked.astype(F32).astype(BF16),
        (i0 <= i1).astype(F32).astype(BF16),
        preferred_element_type=F32,
    )
    rank = jnp.sum(jnp.where(picked, running, 0.0), 0, keepdims=True)
    position = ids_row * SLOTS + rank.astype(jnp.int32) - 1
    aux_row = lax.broadcasted_iota(jnp.int32, (128, rows), 0)
    aux[...] = jnp.where(aux_row == 0, gate, position.astype(F32)).T
    copies.append(pltpu.make_async_copy(aux, aux_ref, sems.at[5]))
    copies[1].start()
    for slot in range(0, experts * SLOTS, block):
        number = lax.broadcasted_iota(jnp.int32, (block, rows), 0) + slot
        spread = (number == position).astype(F32).astype(BF16)
        some = pl.ds(slot // SLOTS, block // SLOTS)
        sent[some] = (
            jnp.dot(spread, normed[...], preferred_element_type=F32)
            .astype(BF16)
            .reshape(block // SLOTS, SLOTS, normed.shape[1])
        )
        copy = pltpu.make_async_copy(sent.at[some], out_ref.at[some], sems.at[slot // block])
        copy.start()
        copies.append(copy)
    wait_all(copies)


def second_half_kernel(
    x_ref, normed_ref, m0, m1, o0, o1, ctx_ref, gain_ref, router_ref, row_ref,
    att_ref, out_ref, aux_ref,
    x, gain, router, ids, w, wo, ctx, projected, normed, sent, att, aux, sems, small,
):
    core = my_core()
    qkv, late = fetch((o0, o1), 1 - core, w, sems.at[0], wo, sems.at[1])
    _, later = fetch((m0, m1), core, None, None, wo, sems.at[2])
    loads = start_all(
        [(x_ref.at[0], x), (gain_ref, gain), (router_ref, router), (row_ref.at[0], ids)], small
    )
    ctx[core] = ctx_ref[...]
    wait_all(qkv)
    project(normed_ref, w.at[1 - core], projected)

    def store(pair, row, context):
        ctx[1 - core, row : row + context.shape[0], pair * 128 : pair * 128 + 128] = context

    attend(projected, store)
    wait_all(late + later + loads)
    finish(x, ctx, wo, gain, router, ids, att_ref, out_ref, aux_ref, normed, sent, att, aux, small)


def whole_kernel(
    x_ref, gain1_ref, m0, m1, o0, o1, gain_ref, router_ref, row_ref,
    att_ref, out_ref, aux_ref,
    gain1, x, gain, router, ids, w, wo, ctx, projected, normed, sent, att, aux, sems, small,
):
    core = my_core()
    first = start_all([(x_ref.at[1], x), (gain1_ref, gain1)], small)
    qkv, late = fetch((m0, m1), core, w, sems.at[0], wo, sems.at[1])
    qkv2, late2 = fetch((o0, o1), 1 - core, w, sems.at[2], wo, sems.at[3])
    loads = start_all(
        [(gain_ref, gain), (router_ref, router), (row_ref.at[1], ids)], small.at[pl.ds(2, 3)]
    )
    wait_all(first)
    normed[...] = scale_rows(x[...], gain1[...]).astype(BF16)
    wait_all(qkv + qkv2)

    def step(side, carry):
        def store(pair, row, context):
            ctx[side, row : row + context.shape[0], pair * 128 : pair * 128 + 128] = context

        project(normed, w.at[side], projected)
        attend(projected, store)
        return carry

    lax.fori_loop(0, 2, step, 0)
    wait_all(late + late2 + loads)
    finish(x, ctx, wo, gain, router, ids, att_ref, out_ref, aux_ref, normed, sent, att, aux, small)


def expert_kernel(x_ref, in_ref, out_ref, y_ref, total, hidden):
    step = pl.program_id(0)
    slots, width = total.shape
    block = 256
    x = x_ref.reshape(slots, width)

    @pl.when(step == 0)
    def _():
        total[...] = jnp.zeros_like(total)

    for at in range(0, slots, block):
        first = jnp.dot(x[at : at + block], in_ref[0], preferred_element_type=F32)
        hidden[at : at + block] = jnp.maximum(first, 0.0).astype(BF16)
    for at in range(0, slots, block):
        total[at : at + block] += jnp.dot(
            hidden[at : at + block], out_ref[0], preferred_element_type=F32
        )

    @pl.when(step == pl.num_programs(0) - 1)
    def _():
        y_ref[...] = total[...].astype(BF16).reshape(y_ref.shape)


def combine_kernel(batch, att_ref, aux_ref, back_ref, out_ref, att, aux, done, sems):
    rows, width = att.shape
    slots = back_ref.shape[0] * SLOTS
    block = 128
    back = back_ref.reshape(slots, width)
    loads = start_all([(aux_ref, aux), (att_ref, att)], sems.at[pl.ds(4, 2)])
    loads[0].wait()
    copies = []
    for row in range(0, rows, block):
        mine = pl.ds(row, block)
        gate = aux[mine, 0:1]
        position = aux[mine, 1:2].astype(jnp.int32)
        pick = lax.broadcasted_iota(jnp.int32, (block, slots), 1) == position
        result = jnp.dot(pick.astype(F32).astype(BF16), back[...], preferred_element_type=F32)
        if row == 0:
            loads[1].wait()
        done[mine] = (att[mine].astype(F32) + gate * result).astype(BF16)
        copy = pltpu.make_async_copy(done.at[mine], out_ref.at[batch, mine], sems.at[row // block])
        copy.start()
        copies.append(copy)
    wait_all(copies)


def combine_after_kernel(batch, att_ref, aux_ref, back_ref, held_ref, out_ref, *scratch):
    del held_ref
    combine_kernel(batch, att_ref, aux_ref, back_ref, out_ref, *scratch)


def limit(kibibytes):
    return pltpu.CompilerParams(vmem_limit_bytes=kibibytes << 10)


def full(shape):
    return pl.BlockSpec(shape, lambda i: (0,) * len(shape))


def body(
    tokens, expert_ids, attn_qkv, attn_out, norm_attn, norm_ffn, router, expert_in, expert_out
):
    batches, rows, width = tokens.shape
    experts = router.shape[1]
    slots = experts * SLOTS
    core = my_core()
    halves = [
        jnp.concatenate(
            [attn_qkv[:, at + side * HALF : at + side * HALF + HALF] for at in (0, width, 2 * width)]
            + [attn_out[:, side * HALF : side * HALF + HALF]],
            axis=1,
        )
        for side in range(2)
    ]
    piece = jnp.where(core == 0, halves[0], halves[1])
    swap = [(i, i ^ 1) for i in range(128)]
    steps = (1, -1, 2)
    own = jnp.concatenate([piece] + [lax.ppermute(piece, ALL, hop(d, 0)) for d in steps], axis=0)
    rest = jnp.concatenate([lax.ppermute(own, ALL, hop(d, 1)) for d in steps], axis=0)
    mine = [own, rest]
    other = [lax.ppermute(part, ALL, swap) for part in mine]
    mine = [pltpu.with_memory_space_constraint(part, pltpu.VMEM) for part in mine]
    other = [pltpu.with_memory_space_constraint(part, pltpu.VMEM) for part in other]

    ids_row = expert_ids.reshape(batches, 1, rows)

    any_spec = pl.BlockSpec(memory_space=pltpu.HBM)
    whole = pl.BlockSpec(memory_space=pltpu.VMEM)

    def near(value):
        return pltpu.with_memory_space_constraint(value, pltpu.VMEM)

    def far(value):
        return pltpu.with_memory_space_constraint(value, pltpu.HBM)

    w_scratch = pltpu.VMEM((2, width, 3 * HALF), BF16)
    projected = pltpu.VMEM((rows, 3 * HALF), BF16)
    one = pltpu.VMEM((rows, width), BF16)
    gain_scratch = pltpu.VMEM((width,), F32)
    ctx_mine, normed = pl.pallas_call(
        context_kernel,
        out_shape=(
            jax.ShapeDtypeStruct((rows, HALF), BF16),
            jax.ShapeDtypeStruct((rows, width), BF16),
        ),
        in_specs=[any_spec] * 2 + [whole] * 2,
        out_specs=(whole, whole),
        scratch_shapes=[
            one,
            gain_scratch,
            w_scratch,
            projected,
            pltpu.SemaphoreType.DMA((16,)),
            pltpu.SemaphoreType.DMA((2,)),
        ],
        compiler_params=limit(47104),
        name="first_half",
    )(tokens, norm_attn, *mine)

    finish_out = (
        jax.ShapeDtypeStruct((rows, width), BF16),
        jax.ShapeDtypeStruct((experts, SLOTS, width), BF16),
        jax.ShapeDtypeStruct((rows, 128), F32),
    )
    finish_specs = (any_spec, any_spec, any_spec)
    scratch = [
        one,
        gain_scratch,
        pltpu.VMEM((width, experts), BF16),
        pltpu.VMEM((1, rows), jnp.int32),
        w_scratch,
        pltpu.VMEM((width, width), BF16),
        pltpu.VMEM((2, rows, HALF), BF16),
        projected,
        one,
        pltpu.VMEM((experts, SLOTS, width), BF16),
        one,
        pltpu.VMEM((rows, 128), F32),
        pltpu.SemaphoreType.DMA((4, 16)),
        pltpu.SemaphoreType.DMA((6,)),
    ]

    first = pl.pallas_call(
        second_half_kernel,
        out_shape=finish_out,
        in_specs=[any_spec] + [whole] * 6 + [any_spec] * 3,
        out_specs=finish_specs,
        scratch_shapes=scratch,
        compiler_params=limit(55900),
        name="second_half",
    )(tokens, near(normed), *mine, *other, near(ctx_mine), norm_ffn, router, ids_row)

    second = pl.pallas_call(
        whole_kernel,
        out_shape=finish_out,
        in_specs=[any_spec] * 2 + [whole] * 4 + [any_spec] * 3,
        out_specs=finish_specs,
        scratch_shapes=[gain_scratch] + scratch,
        compiler_params=limit(55500),
        name="whole",
    )(tokens, norm_attn, *mine, *other, norm_ffn, router, ids_row)

    def exchange(values):
        moved = lax.all_to_all(values, ALL, split_axis=0, concat_axis=0, tiled=True)
        return pltpu.with_memory_space_constraint(moved, pltpu.VMEM)

    hidden = expert_in.shape[2]
    chunk = 512
    def serve(values):
        return pl.pallas_call(
            expert_kernel,
            grid=(hidden // chunk,),
            out_shape=jax.ShapeDtypeStruct((experts, SLOTS, width), BF16),
            in_specs=[
                whole,
                pl.BlockSpec((1, width, chunk), lambda j: (0, 0, j)),
                pl.BlockSpec((1, chunk, width), lambda j: (0, j, 0)),
            ],
            out_specs=pl.BlockSpec((experts, SLOTS, width), lambda j: (0, 0, 0)),
            scratch_shapes=[pltpu.VMEM((slots, width), F32), pltpu.VMEM((slots, chunk), BF16)],
            compiler_params=limit(58300),
            name="expert",
        )(values, far(expert_in), far(expert_out))

    arrived = [exchange(first[1]), exchange(second[1])]
    back = [exchange(serve(values)) for values in arrived]

    out_shape = jax.ShapeDtypeStruct((batches, rows, width), BF16)
    combine_scratch = [
        one,
        pltpu.VMEM((rows, 128), F32),
        one,
        pltpu.SemaphoreType.DMA((6,)),
    ]
    held = pl.pallas_call(
        functools.partial(combine_kernel, 0),
        out_shape=out_shape,
        in_specs=[any_spec] * 2 + [whole],
        out_specs=any_spec,
        scratch_shapes=combine_scratch,
        compiler_params=limit(58300),
        name="combine0",
    )(first[0], first[2], back[0])
    return pl.pallas_call(
        functools.partial(combine_after_kernel, 1),
        out_shape=out_shape,
        in_specs=[any_spec] * 2 + [whole, any_spec],
        out_specs=any_spec,
        scratch_shapes=combine_scratch,
        input_output_aliases={3: 0},
        compiler_params=limit(58300),
        name="combine1",
    )(second[0], second[2], back[1], held)


def solution(mesh):
    in_specs = (
        P(None, ALL, None),
        P(None, ALL, None),
        P(("seq", "role"), None),
        P(("seq", "role"), None),
        P(),
        P(),
        P(),
        P(ALL, None, None),
        P(ALL, None, None),
    )
    return jax.shard_map(
        body, mesh=mesh, in_specs=in_specs, out_specs=P(None, ALL, None), check_vma=False
    )
```

```python
import functools

import jax
import jax.numpy as jnp
from jax import lax
from jax.experimental import pallas as pl
from jax.experimental.pallas import tpu as pltpu
from jax.sharding import PartitionSpec as P

HEADS = 12
HALF = 384
SLOTS = 8
ALL = ("seq", "role", "exp")
F32 = jnp.float32
BF16 = jnp.bfloat16


def place(x, z, y, c):
    return x * 32 + z * 8 + y * 2 + c


def hop(d, phase):
    pairs = []
    for x in range(4):
        for z in range(4):
            for y in range(4):
                for c in range(2):
                    if (c == 0) == (phase == 0):
                        to = place((x + d) % 4, z, y, c)
                    else:
                        to = place(x, (z + d) % 4, y, c)
                    pairs.append((place(x, z, y, c), to))
    return pairs


def my_core():
    return lax.rem(lax.axis_index("exp"), 2)


def scale_rows(values, gain):
    floats = values.astype(F32)
    return floats * lax.rsqrt(jnp.mean(floats * floats, -1, keepdims=True) + 1e-06) * gain


def fetch(blocks, core, w, sem, wo=None, wo_sem=None):
    own, rest = blocks
    seq = lax.axis_index("seq")
    x = seq // 2
    z = lax.rem(seq, 2) * 2 + lax.axis_index("role")
    shift = (0, 3, 1, 2)
    copies, late = [], []
    for i in range(4):
        for j in range(4):
            source, at = (own, j * 48) if i == 0 else (rest, (i * 4 + j - 4) * 48)
            dx = jnp.where(core == 0, shift[j], shift[i])
            dz = jnp.where(core == 0, shift[i], shift[j])
            row = (lax.rem(x + dx, 4) * 4 + lax.rem(z + dz, 4)) * 48
            row = pl.multiple_of(row, 16)
            if w is not None:
                copies.append(
                    pltpu.make_async_copy(
                        source.at[pl.ds(at, 48), pl.ds(0, 3 * HALF)],
                        w.at[core, pl.ds(row, 48), :],
                        sem.at[i * 4 + j],
                    )
                )
            if wo is not None:
                late.append(
                    pltpu.make_async_copy(
                        source.at[pl.ds(at, 48), pl.ds(3 * HALF, HALF)],
                        wo.at[pl.ds(row, 48), pl.ds(pl.multiple_of(core * HALF, 128), HALF)],
                        wo_sem.at[i * 4 + j],
                    )
                )
    for copy in copies + late:
        copy.start()
    return copies, late


def wait_all(copies):
    for copy in copies:
        copy.wait()


def project(normed, weights, projected):
    projected[...] = jnp.dot(normed[...], weights[...], preferred_element_type=F32).astype(BF16)


def start_all(pairs, sems):
    copies = [
        pltpu.make_async_copy(source, target, sems.at[i]) for i, (source, target) in enumerate(pairs)
    ]
    for copy in copies:
        copy.start()
    return copies


def attend(projected, store):
    rows = projected.shape[0]
    block = 256
    low = lax.broadcasted_iota(jnp.int32, (block, 128), 1) < 64
    for pair in range(3):
        at = pair * 128
        k = projected[:, HALF + at : HALF + at + 128]
        v = projected[:, 2 * HALF + at : 2 * HALF + at + 128]
        values = jnp.concatenate([v, jnp.ones((rows, 128), BF16)], axis=1)
        for row in range(0, rows, block):
            q = projected[row : row + block, at : at + 128] * jnp.asarray(0.125, BF16)
            zero = jnp.zeros_like(q)
            outs = []
            for side in range(2):
                mine = jnp.where(low, q, zero) if side == 0 else jnp.where(low, zero, q)
                scores = lax.dot_general(
                    mine, k, (((1,), (1,)), ((), ())), preferred_element_type=F32
                )
                weight = jnp.exp(scores - jnp.max(scores, -1, keepdims=True)).astype(BF16)
                total = jnp.dot(weight, values, preferred_element_type=F32)
                outs.append(total[:, :128] / total[:, 128:])
            store(pair, row, jnp.where(low, outs[0], outs[1]).astype(BF16))


def context_kernel(
    x_ref, gain_ref, b0, b1, ctx_ref, normed_ref, x, gain, w, projected, sem, small
):
    core = my_core()
    loads = start_all([(x_ref.at[0], x), (gain_ref, gain)], small)
    copies, _ = fetch((b0, b1), core, w, sem)
    wait_all(loads)
    normed_ref[...] = scale_rows(x[...], gain[...]).astype(BF16)
    wait_all(copies)
    project(normed_ref, w.at[core], projected)

    def store(pair, row, context):
        ctx_ref[row : row + context.shape[0], pair * 128 : pair * 128 + 128] = context

    attend(projected, store)


def finish(
    x, ctx, wo, gain, router, ids, att_ref, out_ref, aux_ref, normed, sent, att, aux, sems
):
    rows, experts = x.shape[0], router.shape[1]
    block = 256
    for row in range(0, rows, block):
        mine = slice(row, row + block)
        both = jnp.concatenate([ctx[0, mine], ctx[1, mine]], axis=1)
        mixed = jnp.dot(both, wo[...], preferred_element_type=F32)
        attended = (x[mine].astype(F32) + mixed).astype(BF16)
        att[mine] = attended
        normed[mine] = scale_rows(attended, gain[...]).astype(BF16)
    copies = [pltpu.make_async_copy(att, att_ref, sems.at[4])]
    copies[0].start()
    ids_row = ids[...]
    logits = lax.dot_general(
        router[...], normed[...], (((0,), (1,)), ((), ())), preferred_element_type=F32
    )
    i0 = lax.broadcasted_iota(jnp.int32, (rows, rows), 0)
    i1 = lax.broadcasted_iota(jnp.int32, (rows, rows), 1)
    picked = ids_row == lax.broadcasted_iota(jnp.int32, (experts, rows), 0)
    gate = jax.nn.sigmoid(jnp.sum(jnp.where(picked, logits, 0.0), 0, keepdims=True))
    running = jnp.dot(
        picked.astype(F32).astype(BF16),
        (i0 <= i1).astype(F32).astype(BF16),
        preferred_element_type=F32,
    )
    rank = jnp.sum(jnp.where(picked, running, 0.0), 0, keepdims=True)
    position = ids_row * SLOTS + rank.astype(jnp.int32) - 1
    aux_row = lax.broadcasted_iota(jnp.int32, (128, rows), 0)
    aux[...] = jnp.where(aux_row == 0, gate, position.astype(F32)).T
    copies.append(pltpu.make_async_copy(aux, aux_ref, sems.at[5]))
    copies[1].start()
    for slot in range(0, experts * SLOTS, block):
        number = lax.broadcasted_iota(jnp.int32, (block, rows), 0) + slot
        spread = (number == position).astype(F32).astype(BF16)
        some = pl.ds(slot // SLOTS, block // SLOTS)
        sent[some] = (
            jnp.dot(spread, normed[...], preferred_element_type=F32)
            .astype(BF16)
            .reshape(block // SLOTS, SLOTS, normed.shape[1])
        )
        copy = pltpu.make_async_copy(sent.at[some], out_ref.at[some], sems.at[slot // block])
        copy.start()
        copies.append(copy)
    wait_all(copies)


def second_half_kernel(
    x_ref, normed_ref, m0, m1, o0, o1, ctx_ref, gain_ref, router_ref, row_ref,
    att_ref, out_ref, aux_ref,
    x, gain, router, ids, w, wo, ctx, projected, normed, sent, att, aux, sems, small,
):
    core = my_core()
    qkv, late = fetch((o0, o1), 1 - core, w, sems.at[0], wo, sems.at[1])
    _, later = fetch((m0, m1), core, None, None, wo, sems.at[2])
    loads = start_all(
        [(x_ref.at[0], x), (gain_ref, gain), (router_ref, router), (row_ref.at[0], ids)], small
    )
    ctx[core] = ctx_ref[...]
    wait_all(qkv)
    project(normed_ref, w.at[1 - core], projected)

    def store(pair, row, context):
        ctx[1 - core, row : row + context.shape[0], pair * 128 : pair * 128 + 128] = context

    attend(projected, store)
    wait_all(late + later + loads)
    finish(x, ctx, wo, gain, router, ids, att_ref, out_ref, aux_ref, normed, sent, att, aux, small)


def whole_kernel(
    x_ref, gain1_ref, m0, m1, o0, o1, gain_ref, router_ref, row_ref,
    att_ref, out_ref, aux_ref,
    gain1, x, gain, router, ids, w, wo, ctx, projected, normed, sent, att, aux, sems, small,
):
    core = my_core()
    first = start_all([(x_ref.at[1], x), (gain1_ref, gain1)], small)
    qkv, late = fetch((m0, m1), core, w, sems.at[0], wo, sems.at[1])
    qkv2, late2 = fetch((o0, o1), 1 - core, w, sems.at[2], wo, sems.at[3])
    loads = start_all(
        [(gain_ref, gain), (router_ref, router), (row_ref.at[1], ids)], small.at[pl.ds(2, 3)]
    )
    wait_all(first)
    normed[...] = scale_rows(x[...], gain1[...]).astype(BF16)
    wait_all(qkv + qkv2)

    def step(side, carry):
        def store(pair, row, context):
            ctx[side, row : row + context.shape[0], pair * 128 : pair * 128 + 128] = context

        project(normed, w.at[side], projected)
        attend(projected, store)
        return carry

    lax.fori_loop(0, 2, step, 0)
    wait_all(late + late2 + loads)
    finish(x, ctx, wo, gain, router, ids, att_ref, out_ref, aux_ref, normed, sent, att, aux, small)


def expert_kernel(x_ref, in_ref, out_ref, y_ref, total, hidden):
    step = pl.program_id(0)
    slots, width = total.shape
    block = 256
    x = x_ref.reshape(slots, width)

    @pl.when(step == 0)
    def _():
        total[...] = jnp.zeros_like(total)

    for at in range(0, slots, block):
        first = jnp.dot(x[at : at + block], in_ref[0], preferred_element_type=F32)
        hidden[at : at + block] = jnp.maximum(first, 0.0).astype(BF16)
    for at in range(0, slots, block):
        total[at : at + block] += jnp.dot(
            hidden[at : at + block], out_ref[0], preferred_element_type=F32
        )

    @pl.when(step == pl.num_programs(0) - 1)
    def _():
        y_ref[...] = total[...].astype(BF16).reshape(y_ref.shape)


def combine_kernel(batch, att_ref, aux_ref, back_ref, out_ref, att, aux, done, sems):
    rows, width = att.shape
    slots = back_ref.shape[0] * SLOTS
    block = 128
    back = back_ref.reshape(slots, width)
    loads = start_all([(aux_ref, aux), (att_ref, att)], sems.at[pl.ds(4, 2)])
    loads[0].wait()
    copies = []
    for row in range(0, rows, block):
        mine = pl.ds(row, block)
        gate = aux[mine, 0:1]
        position = aux[mine, 1:2].astype(jnp.int32)
        pick = lax.broadcasted_iota(jnp.int32, (block, slots), 1) == position
        result = jnp.dot(pick.astype(F32).astype(BF16), back[...], preferred_element_type=F32)
        if row == 0:
            loads[1].wait()
        done[mine] = (att[mine].astype(F32) + gate * result).astype(BF16)
        copy = pltpu.make_async_copy(done.at[mine], out_ref.at[batch, mine], sems.at[row // block])
        copy.start()
        copies.append(copy)
    wait_all(copies)


def combine_after_kernel(batch, att_ref, aux_ref, back_ref, held_ref, out_ref, *scratch):
    del held_ref
    combine_kernel(batch, att_ref, aux_ref, back_ref, out_ref, *scratch)


def limit(kibibytes):
    return pltpu.CompilerParams(vmem_limit_bytes=kibibytes << 10)


def full(shape):
    return pl.BlockSpec(shape, lambda i: (0,) * len(shape))


def body(
    tokens, expert_ids, attn_qkv, attn_out, norm_attn, norm_ffn, router, expert_in, expert_out
):
    batches, rows, width = tokens.shape
    experts = router.shape[1]
    slots = experts * SLOTS
    core = my_core()
    halves = [
        jnp.concatenate(
            [attn_qkv[:, at + side * HALF : at + side * HALF + HALF] for at in (0, width, 2 * width)]
            + [attn_out[:, side * HALF : side * HALF + HALF]],
            axis=1,
        )
        for side in range(2)
    ]
    piece = jnp.where(core == 0, halves[0], halves[1])
    swap = [(i, i ^ 1) for i in range(128)]
    steps = (1, -1, 2)
    own = jnp.concatenate([piece] + [lax.ppermute(piece, ALL, hop(d, 0)) for d in steps], axis=0)
    rest = jnp.concatenate([lax.ppermute(own, ALL, hop(d, 1)) for d in steps], axis=0)
    mine = [own, rest]
    other = [lax.ppermute(part, ALL, swap) for part in mine]
    mine = [pltpu.with_memory_space_constraint(part, pltpu.VMEM) for part in mine]
    other = [pltpu.with_memory_space_constraint(part, pltpu.VMEM) for part in other]

    ids_row = expert_ids.reshape(batches, 1, rows)

    any_spec = pl.BlockSpec(memory_space=pltpu.HBM)
    whole = pl.BlockSpec(memory_space=pltpu.VMEM)

    def near(value):
        return pltpu.with_memory_space_constraint(value, pltpu.VMEM)

    def far(value):
        return pltpu.with_memory_space_constraint(value, pltpu.HBM)

    w_scratch = pltpu.VMEM((2, width, 3 * HALF), BF16)
    projected = pltpu.VMEM((rows, 3 * HALF), BF16)
    one = pltpu.VMEM((rows, width), BF16)
    gain_scratch = pltpu.VMEM((width,), F32)
    ctx_mine, normed = pl.pallas_call(
        context_kernel,
        out_shape=(
            jax.ShapeDtypeStruct((rows, HALF), BF16),
            jax.ShapeDtypeStruct((rows, width), BF16),
        ),
        in_specs=[any_spec] * 2 + [whole] * 2,
        out_specs=(whole, whole),
        scratch_shapes=[
            one,
            gain_scratch,
            w_scratch,
            projected,
            pltpu.SemaphoreType.DMA((16,)),
            pltpu.SemaphoreType.DMA((2,)),
        ],
        compiler_params=limit(47104),
        name="first_half",
    )(tokens, norm_attn, *mine)

    finish_out = (
        jax.ShapeDtypeStruct((rows, width), BF16),
        jax.ShapeDtypeStruct((experts, SLOTS, width), BF16),
        jax.ShapeDtypeStruct((rows, 128), F32),
    )
    finish_specs = (any_spec, any_spec, any_spec)
    scratch = [
        one,
        gain_scratch,
        pltpu.VMEM((width, experts), BF16),
        pltpu.VMEM((1, rows), jnp.int32),
        w_scratch,
        pltpu.VMEM((width, width), BF16),
        pltpu.VMEM((2, rows, HALF), BF16),
        projected,
        one,
        pltpu.VMEM((experts, SLOTS, width), BF16),
        one,
        pltpu.VMEM((rows, 128), F32),
        pltpu.SemaphoreType.DMA((4, 16)),
        pltpu.SemaphoreType.DMA((6,)),
    ]

    first = pl.pallas_call(
        second_half_kernel,
        out_shape=finish_out,
        in_specs=[any_spec] + [whole] * 6 + [any_spec] * 3,
        out_specs=finish_specs,
        scratch_shapes=scratch,
        compiler_params=limit(54000),
        name="second_half",
    )(tokens, near(normed), *mine, *other, near(ctx_mine), norm_ffn, router, ids_row)

    second = pl.pallas_call(
        whole_kernel,
        out_shape=finish_out,
        in_specs=[any_spec] * 2 + [whole] * 4 + [any_spec] * 3,
        out_specs=finish_specs,
        scratch_shapes=[gain_scratch] + scratch,
        compiler_params=limit(54000),
        name="whole",
    )(tokens, norm_attn, *mine, *other, norm_ffn, router, ids_row)

    def exchange(values):
        moved = lax.all_to_all(values, ALL, split_axis=0, concat_axis=0, tiled=True)
        return pltpu.with_memory_space_constraint(moved, pltpu.VMEM)

    hidden = expert_in.shape[2]
    chunk = 512
    def serve(values):
        return pl.pallas_call(
            expert_kernel,
            grid=(hidden // chunk,),
            out_shape=jax.ShapeDtypeStruct((experts, SLOTS, width), BF16),
            in_specs=[
                whole,
                pl.BlockSpec((1, width, chunk), lambda j: (0, 0, j)),
                pl.BlockSpec((1, chunk, width), lambda j: (0, j, 0)),
            ],
            out_specs=pl.BlockSpec((experts, SLOTS, width), lambda j: (0, 0, 0)),
            scratch_shapes=[pltpu.VMEM((slots, width), F32), pltpu.VMEM((slots, chunk), BF16)],
            compiler_params=limit(58300),
            name="expert",
        )(values, far(expert_in), far(expert_out))

    arrived = [exchange(first[1]), exchange(second[1])]
    back = [exchange(serve(values)) for values in arrived]

    out_shape = jax.ShapeDtypeStruct((batches, rows, width), BF16)
    combine_scratch = [
        one,
        pltpu.VMEM((rows, 128), F32),
        one,
        pltpu.SemaphoreType.DMA((6,)),
    ]
    held = pl.pallas_call(
        functools.partial(combine_kernel, 0),
        out_shape=out_shape,
        in_specs=[any_spec] * 2 + [whole],
        out_specs=any_spec,
        scratch_shapes=combine_scratch,
        compiler_params=limit(58300),
        name="combine0",
    )(first[0], first[2], back[0])
    return pl.pallas_call(
        functools.partial(combine_after_kernel, 1),
        out_shape=out_shape,
        in_specs=[any_spec] * 2 + [whole, any_spec],
        out_specs=any_spec,
        scratch_shapes=combine_scratch,
        input_output_aliases={3: 0},
        compiler_params=limit(58300),
        name="combine1",
    )(second[0], second[2], back[1], held)


def solution(mesh):
    in_specs = (
        P(None, ALL, None),
        P(None, ALL, None),
        P(("seq", "role"), None),
        P(("seq", "role"), None),
        P(),
        P(),
        P(),
        P(ALL, None, None),
        P(ALL, None, None),
    )
    return jax.shard_map(
        body, mesh=mesh, in_specs=in_specs, out_specs=P(None, ALL, None), check_vma=False
    )
```

```python
import functools

import jax
import jax.numpy as jnp
from jax import lax
from jax.experimental import pallas as pl
from jax.experimental.pallas import tpu as pltpu
from jax.sharding import PartitionSpec as P

HEADS = 12
HALF = 384
EXPERTS = 128
SLOTS = 8
ALL = ("seq", "role", "exp")
F32 = jnp.float32
BF16 = jnp.bfloat16


def place(x, z, y, c):
    return x * 32 + z * 8 + y * 2 + c


def hop(d, phase):
    pairs = []
    for x in range(4):
        for z in range(4):
            for y in range(4):
                for c in range(2):
                    if (c == 0) == (phase == 0):
                        to = place((x + d) % 4, z, y, c)
                    else:
                        to = place(x, (z + d) % 4, y, c)
                    pairs.append((place(x, z, y, c), to))
    return pairs


def my_core():
    return lax.rem(lax.axis_index("exp"), 2)


def scale_rows(values, gain):
    floats = values.astype(F32)
    return floats * lax.rsqrt(jnp.mean(floats * floats, -1, keepdims=True) + 1e-06) * gain


def fetch(blocks, core, w, sem, wo=None, wo_sem=None):
    own, rest = blocks
    seq = lax.axis_index("seq")
    x = seq // 2
    z = lax.rem(seq, 2) * 2 + lax.axis_index("role")
    shift = (0, 3, 1, 2)
    copies, late = [], []
    for i in range(4):
        for j in range(4):
            source, at = (own, j * 48) if i == 0 else (rest, (i * 4 + j - 4) * 48)
            dx = jnp.where(core == 0, shift[j], shift[i])
            dz = jnp.where(core == 0, shift[i], shift[j])
            row = (lax.rem(x + dx, 4) * 4 + lax.rem(z + dz, 4)) * 48
            row = pl.multiple_of(row, 16)
            if w is not None:
                copies.append(
                    pltpu.make_async_copy(
                        source.at[pl.ds(at, 48), pl.ds(0, 3 * HALF)],
                        w.at[core, pl.ds(row, 48), :],
                        sem.at[i * 4 + j],
                    )
                )
            if wo is not None:
                late.append(
                    pltpu.make_async_copy(
                        source.at[pl.ds(at, 48), pl.ds(3 * HALF, HALF)],
                        wo.at[pl.ds(row, 48), pl.ds(pl.multiple_of(core * HALF, 128), HALF)],
                        wo_sem.at[i * 4 + j],
                    )
                )
    for copy in copies + late:
        copy.start()
    return copies, late


def wait_all(copies):
    for copy in copies:
        copy.wait()


def project(normed, weights, projected):
    projected[...] = jnp.dot(normed[...], weights[...], preferred_element_type=F32).astype(BF16)


def start_all(pairs, sems):
    copies = [
        pltpu.make_async_copy(source, target, sems.at[i]) for i, (source, target) in enumerate(pairs)
    ]
    for copy in copies:
        copy.start()
    return copies


def attend(projected, store):
    rows = projected.shape[0]
    block = 256
    low = lax.broadcasted_iota(jnp.int32, (block, 128), 1) < 64
    for pair in range(3):
        at = pair * 128
        k = projected[:, HALF + at : HALF + at + 128]
        v = projected[:, 2 * HALF + at : 2 * HALF + at + 128]
        values = jnp.concatenate([v, jnp.ones((rows, 128), BF16)], axis=1)
        for row in range(0, rows, block):
            q = projected[row : row + block, at : at + 128] * jnp.asarray(0.125, BF16)
            zero = jnp.zeros_like(q)
            outs = []
            for side in range(2):
                mine = jnp.where(low, q, zero) if side == 0 else jnp.where(low, zero, q)
                scores = lax.dot_general(
                    mine, k, (((1,), (1,)), ((), ())), preferred_element_type=F32
                )
                weight = jnp.exp(scores - jnp.max(scores, -1, keepdims=True)).astype(BF16)
                total = jnp.dot(weight, values, preferred_element_type=F32)
                outs.append(total[:, :128] / total[:, 128:])
            store(pair, row, jnp.where(low, outs[0], outs[1]).astype(BF16))


def prepare_kernel(x_ref, gain_ref, row_ref, normed_ref, position_ref):
    rows = x_ref.shape[1]
    normed_ref[0] = scale_rows(x_ref[0], gain_ref[...]).astype(BF16)
    ids_row = row_ref[0]
    i0 = lax.broadcasted_iota(jnp.int32, (rows, rows), 0)
    i1 = lax.broadcasted_iota(jnp.int32, (rows, rows), 1)
    picked = ids_row == lax.broadcasted_iota(jnp.int32, (EXPERTS, rows), 0)
    running = jnp.dot(
        picked.astype(F32).astype(BF16),
        (i0 <= i1).astype(F32).astype(BF16),
        preferred_element_type=F32,
    )
    rank = jnp.sum(jnp.where(picked, running, 0.0), 0, keepdims=True)
    position_ref[0] = ids_row * SLOTS + rank.astype(jnp.int32) - 1


def context_kernel(n_ref, b0, b1, ctx_ref, normed, w, projected, sem, small):
    core = my_core()
    loads = start_all([(n_ref.at[0], normed)], small)
    copies, _ = fetch((b0, b1), core, w, sem)
    wait_all(loads + copies)
    project(normed, w.at[core], projected)

    def store(pair, row, context):
        ctx_ref[row : row + context.shape[0], pair * 128 : pair * 128 + 128] = context

    attend(projected, store)


def finish(
    x, ctx, wo, gain, router, ids, place_row, att_ref, out_ref, aux_ref, normed, sent, att, aux, sems
):
    rows, experts = x.shape[0], router.shape[1]
    block = 256
    for row in range(0, rows, block):
        mine = slice(row, row + block)
        both = jnp.concatenate([ctx[0, mine], ctx[1, mine]], axis=1)
        mixed = jnp.dot(both, wo[...], preferred_element_type=F32)
        attended = (x[mine].astype(F32) + mixed).astype(BF16)
        att[mine] = attended
        normed[mine] = scale_rows(attended, gain[...]).astype(BF16)
    copies = [pltpu.make_async_copy(att, att_ref, sems.at[4])]
    copies[0].start()
    ids_row = ids[...]
    logits = lax.dot_general(
        router[...], normed[...], (((0,), (1,)), ((), ())), preferred_element_type=F32
    )
    picked = ids_row == lax.broadcasted_iota(jnp.int32, (experts, rows), 0)
    gate = jax.nn.sigmoid(jnp.sum(jnp.where(picked, logits, 0.0), 0, keepdims=True))
    position = place_row[...]
    aux_row = lax.broadcasted_iota(jnp.int32, (128, rows), 0)
    aux[...] = jnp.where(aux_row == 0, gate, position.astype(F32)).T
    copies.append(pltpu.make_async_copy(aux, aux_ref, sems.at[5]))
    copies[1].start()
    for slot in range(0, experts * SLOTS, block):
        number = lax.broadcasted_iota(jnp.int32, (block, rows), 0) + slot
        spread = (number == position).astype(F32).astype(BF16)
        some = pl.ds(slot // SLOTS, block // SLOTS)
        sent[some] = (
            jnp.dot(spread, normed[...], preferred_element_type=F32)
            .astype(BF16)
            .reshape(block // SLOTS, SLOTS, normed.shape[1])
        )
        copy = pltpu.make_async_copy(sent.at[some], out_ref.at[some], sems.at[slot // block])
        copy.start()
        copies.append(copy)
    wait_all(copies)


def second_half_kernel(
    x_ref, n_ref, m0, m1, o0, o1, ctx_ref, gain_ref, router_ref, row_ref, position_ref,
    att_ref, out_ref, aux_ref,
    x, gain, router, ids, place_row, w, wo, ctx, projected, normed, sent, att, aux, sems, small,
):
    core = my_core()
    qkv, late = fetch((o0, o1), 1 - core, w, sems.at[0], wo, sems.at[1])
    _, later = fetch((m0, m1), core, None, None, wo, sems.at[2])
    loads = start_all(
        [
            (x_ref.at[0], x), (gain_ref, gain), (router_ref, router), (row_ref.at[0], ids),
            (position_ref.at[0], place_row),
        ],
        small,
    )
    ctx[core] = ctx_ref[...]
    wait_all(qkv)
    project(n_ref, w.at[1 - core], projected)

    def store(pair, row, context):
        ctx[1 - core, row : row + context.shape[0], pair * 128 : pair * 128 + 128] = context

    attend(projected, store)
    wait_all(late + later + loads)
    finish(
        x, ctx, wo, gain, router, ids, place_row, att_ref, out_ref, aux_ref,
        normed, sent, att, aux, small,
    )


def whole_kernel(
    x_ref, n_ref, m0, m1, o0, o1, gain_ref, router_ref, row_ref, position_ref,
    att_ref, out_ref, aux_ref,
    x, gain, router, ids, place_row, w, wo, ctx, projected, normed, sent, att, aux, sems, small,
):
    core = my_core()
    first = start_all([(n_ref.at[1], normed)], small.at[pl.ds(5, 1)])
    qkv, late = fetch((m0, m1), core, w, sems.at[0], wo, sems.at[1])
    qkv2, late2 = fetch((o0, o1), 1 - core, w, sems.at[2], wo, sems.at[3])
    loads = start_all(
        [
            (x_ref.at[1], x), (gain_ref, gain), (router_ref, router), (row_ref.at[1], ids),
            (position_ref.at[1], place_row),
        ],
        small,
    )
    wait_all(first + qkv + qkv2)

    def step(side, carry):
        def store(pair, row, context):
            ctx[side, row : row + context.shape[0], pair * 128 : pair * 128 + 128] = context

        project(normed, w.at[side], projected)
        attend(projected, store)
        return carry

    lax.fori_loop(0, 2, step, 0)
    wait_all(late + late2 + loads)
    finish(
        x, ctx, wo, gain, router, ids, place_row, att_ref, out_ref, aux_ref,
        normed, sent, att, aux, small,
    )


def expert_kernel(x_ref, in_ref, out_ref, y_ref, total, hidden):
    step = pl.program_id(0)
    slots, width = total.shape
    block = 256
    x = x_ref.reshape(slots, width)

    @pl.when(step == 0)
    def _():
        total[...] = jnp.zeros_like(total)

    for at in range(0, slots, block):
        first = jnp.dot(x[at : at + block], in_ref[0], preferred_element_type=F32)
        hidden[at : at + block] = jnp.maximum(first, 0.0).astype(BF16)
    for at in range(0, slots, block):
        total[at : at + block] += jnp.dot(
            hidden[at : at + block], out_ref[0], preferred_element_type=F32
        )

    @pl.when(step == pl.num_programs(0) - 1)
    def _():
        y_ref[...] = total[...].astype(BF16).reshape(y_ref.shape)


def combine_kernel(batch, att_ref, aux_ref, back_ref, out_ref, att, aux, done, sems):
    rows, width = att.shape
    slots = back_ref.shape[0] * SLOTS
    block = 128
    back = back_ref.reshape(slots, width)
    loads = start_all([(aux_ref, aux), (att_ref, att)], sems.at[pl.ds(4, 2)])
    loads[0].wait()
    copies = []
    for row in range(0, rows, block):
        mine = pl.ds(row, block)
        gate = aux[mine, 0:1]
        position = aux[mine, 1:2].astype(jnp.int32)
        pick = lax.broadcasted_iota(jnp.int32, (block, slots), 1) == position
        result = jnp.dot(pick.astype(F32).astype(BF16), back[...], preferred_element_type=F32)
        if row == 0:
            loads[1].wait()
        done[mine] = (att[mine].astype(F32) + gate * result).astype(BF16)
        copy = pltpu.make_async_copy(done.at[mine], out_ref.at[batch, mine], sems.at[row // block])
        copy.start()
        copies.append(copy)
    wait_all(copies)


def combine_after_kernel(batch, att_ref, aux_ref, back_ref, held_ref, out_ref, *scratch):
    del held_ref
    combine_kernel(batch, att_ref, aux_ref, back_ref, out_ref, *scratch)


def limit(kibibytes):
    return pltpu.CompilerParams(vmem_limit_bytes=kibibytes << 10)


def full(shape):
    return pl.BlockSpec(shape, lambda i: (0,) * len(shape))


def body(
    tokens, expert_ids, attn_qkv, attn_out, norm_attn, norm_ffn, router, expert_in, expert_out
):
    batches, rows, width = tokens.shape
    experts = router.shape[1]
    slots = experts * SLOTS
    core = my_core()
    halves = [
        jnp.concatenate(
            [attn_qkv[:, at + side * HALF : at + side * HALF + HALF] for at in (0, width, 2 * width)]
            + [attn_out[:, side * HALF : side * HALF + HALF]],
            axis=1,
        )
        for side in range(2)
    ]
    piece = jnp.where(core == 0, halves[0], halves[1])
    swap = [(i, i ^ 1) for i in range(128)]
    steps = (1, -1, 2)
    own = jnp.concatenate([piece] + [lax.ppermute(piece, ALL, hop(d, 0)) for d in steps], axis=0)
    ids_row = expert_ids.reshape(batches, 1, rows)
    normed, position = pl.pallas_call(
        prepare_kernel,
        grid=(batches,),
        out_shape=(
            jax.ShapeDtypeStruct((batches, rows, width), BF16),
            jax.ShapeDtypeStruct((batches, 1, rows), jnp.int32),
        ),
        in_specs=[
            pl.BlockSpec((1, rows, width), lambda b: (b, 0, 0)),
            pl.BlockSpec((width,), lambda b: (0,)),
            pl.BlockSpec((1, 1, rows), lambda b: (b, 0, 0)),
        ],
        out_specs=(
            pl.BlockSpec((1, rows, width), lambda b: (b, 0, 0)),
            pl.BlockSpec((1, 1, rows), lambda b: (b, 0, 0)),
        ),
        compiler_params=limit(47104),
        name="prepare",
    )(tokens, norm_attn, ids_row)
    own, normed, position = lax.optimization_barrier((own, normed, position))
    rest = jnp.concatenate([lax.ppermute(own, ALL, hop(d, 1)) for d in steps], axis=0)
    mine = [own, rest]
    other = [lax.ppermute(part, ALL, swap) for part in mine]
    mine = [pltpu.with_memory_space_constraint(part, pltpu.VMEM) for part in mine]
    other = [pltpu.with_memory_space_constraint(part, pltpu.VMEM) for part in other]

    any_spec = pl.BlockSpec(memory_space=pltpu.HBM)
    whole = pl.BlockSpec(memory_space=pltpu.VMEM)

    def near(value):
        return pltpu.with_memory_space_constraint(value, pltpu.VMEM)

    def far(value):
        return pltpu.with_memory_space_constraint(value, pltpu.HBM)

    w_scratch = pltpu.VMEM((2, width, 3 * HALF), BF16)
    projected = pltpu.VMEM((rows, 3 * HALF), BF16)
    one = pltpu.VMEM((rows, width), BF16)
    gain_scratch = pltpu.VMEM((width,), F32)
    ctx_mine, normed_first = pl.pallas_call(
        context_kernel,
        out_shape=(
            jax.ShapeDtypeStruct((rows, HALF), BF16),
            jax.ShapeDtypeStruct((rows, width), BF16),
        ),
        in_specs=[any_spec] + [whole] * 2,
        out_specs=(whole, whole),
        scratch_shapes=[
            w_scratch,
            projected,
            pltpu.SemaphoreType.DMA((16,)),
            pltpu.SemaphoreType.DMA((1,)),
        ],
        compiler_params=limit(47104),
        name="first_half",
    )(normed, *mine)

    finish_out = (
        jax.ShapeDtypeStruct((rows, width), BF16),
        jax.ShapeDtypeStruct((experts, SLOTS, width), BF16),
        jax.ShapeDtypeStruct((rows, 128), F32),
    )
    finish_specs = (any_spec, any_spec, any_spec)
    scratch = [
        one,
        gain_scratch,
        pltpu.VMEM((width, experts), BF16),
        pltpu.VMEM((1, rows), jnp.int32),
        pltpu.VMEM((1, rows), jnp.int32),
        w_scratch,
        pltpu.VMEM((width, width), BF16),
        pltpu.VMEM((2, rows, HALF), BF16),
        projected,
        one,
        pltpu.VMEM((experts, SLOTS, width), BF16),
        one,
        pltpu.VMEM((rows, 128), F32),
        pltpu.SemaphoreType.DMA((4, 16)),
        pltpu.SemaphoreType.DMA((6,)),
    ]

    first = pl.pallas_call(
        second_half_kernel,
        out_shape=finish_out,
        in_specs=[any_spec] + [whole] * 6 + [any_spec] * 4,
        out_specs=finish_specs,
        scratch_shapes=scratch,
        compiler_params=limit(54000),
        name="second_half",
    )(tokens, near(normed_first), *mine, *other, near(ctx_mine), norm_ffn, router, ids_row, position)

    second = pl.pallas_call(
        whole_kernel,
        out_shape=finish_out,
        in_specs=[any_spec] * 2 + [whole] * 4 + [any_spec] * 4,
        out_specs=finish_specs,
        scratch_shapes=scratch,
        compiler_params=limit(54000),
        name="whole",
    )(tokens, normed, *mine, *other, norm_ffn, router, ids_row, position)

    def exchange(values):
        moved = lax.all_to_all(values, ALL, split_axis=0, concat_axis=0, tiled=True)
        return pltpu.with_memory_space_constraint(moved, pltpu.VMEM)

    hidden = expert_in.shape[2]
    chunk = 512
    def serve(values):
        return pl.pallas_call(
            expert_kernel,
            grid=(hidden // chunk,),
            out_shape=jax.ShapeDtypeStruct((experts, SLOTS, width), BF16),
            in_specs=[
                whole,
                pl.BlockSpec((1, width, chunk), lambda j: (0, 0, j)),
                pl.BlockSpec((1, chunk, width), lambda j: (0, j, 0)),
            ],
            out_specs=pl.BlockSpec((experts, SLOTS, width), lambda j: (0, 0, 0)),
            scratch_shapes=[pltpu.VMEM((slots, width), F32), pltpu.VMEM((slots, chunk), BF16)],
            compiler_params=limit(58300),
            name="expert",
        )(values, far(expert_in), far(expert_out))

    arrived = [exchange(first[1]), exchange(second[1])]
    back = [exchange(serve(values)) for values in arrived]

    out_shape = jax.ShapeDtypeStruct((batches, rows, width), BF16)
    combine_scratch = [
        one,
        pltpu.VMEM((rows, 128), F32),
        one,
        pltpu.SemaphoreType.DMA((6,)),
    ]
    held = pl.pallas_call(
        functools.partial(combine_kernel, 0),
        out_shape=out_shape,
        in_specs=[any_spec] * 2 + [whole],
        out_specs=any_spec,
        scratch_shapes=combine_scratch,
        compiler_params=limit(58300),
        name="combine0",
    )(first[0], first[2], back[0])
    return pl.pallas_call(
        functools.partial(combine_after_kernel, 1),
        out_shape=out_shape,
        in_specs=[any_spec] * 2 + [whole, any_spec],
        out_specs=any_spec,
        scratch_shapes=combine_scratch,
        input_output_aliases={3: 0},
        compiler_params=limit(58300),
        name="combine1",
    )(second[0], second[2], back[1], held)


def solution(mesh):
    in_specs = (
        P(None, ALL, None),
        P(None, ALL, None),
        P(("seq", "role"), None),
        P(("seq", "role"), None),
        P(),
        P(),
        P(),
        P(ALL, None, None),
        P(ALL, None, None),
    )
    return jax.shard_map(
        body, mesh=mesh, in_specs=in_specs, out_specs=P(None, ALL, None), check_vma=False
    )
```

```python
import functools

import jax
import jax.numpy as jnp
from jax import lax
from jax.experimental import pallas as pl
from jax.experimental.pallas import tpu as pltpu
from jax.sharding import PartitionSpec as P

HEADS = 12
HALF = 384
EXPERTS = 128
SLOTS = 8
ALL = ("seq", "role", "exp")
F32 = jnp.float32
BF16 = jnp.bfloat16


def place(x, z, y, c):
    return x * 32 + z * 8 + y * 2 + c


def hop(d, phase):
    pairs = []
    for x in range(4):
        for z in range(4):
            for y in range(4):
                for c in range(2):
                    if (c == 0) == (phase == 0):
                        to = place((x + d) % 4, z, y, c)
                    else:
                        to = place(x, (z + d) % 4, y, c)
                    pairs.append((place(x, z, y, c), to))
    return pairs


def my_core():
    return lax.rem(lax.axis_index("exp"), 2)


def scale_rows(values, gain):
    floats = values.astype(F32)
    return floats * lax.rsqrt(jnp.mean(floats * floats, -1, keepdims=True) + 1e-06) * gain


def fetch(blocks, core, w, sem, wo=None, wo_sem=None):
    own, rest = blocks
    seq = lax.axis_index("seq")
    x = seq // 2
    z = lax.rem(seq, 2) * 2 + lax.axis_index("role")
    shift = (0, 3, 1, 2)
    copies, late = [], []
    for i in range(4):
        for j in range(4):
            source, at = (own, j * 48) if i == 0 else (rest, (i * 4 + j - 4) * 48)
            dx = jnp.where(core == 0, shift[j], shift[i])
            dz = jnp.where(core == 0, shift[i], shift[j])
            row = (lax.rem(x + dx, 4) * 4 + lax.rem(z + dz, 4)) * 48
            row = pl.multiple_of(row, 16)
            if w is not None:
                copies.append(
                    pltpu.make_async_copy(
                        source.at[pl.ds(at, 48), pl.ds(0, 3 * HALF)],
                        w.at[core, pl.ds(row, 48), :],
                        sem.at[i * 4 + j],
                    )
                )
            if wo is not None:
                late.append(
                    pltpu.make_async_copy(
                        source.at[pl.ds(at, 48), pl.ds(3 * HALF, HALF)],
                        wo.at[pl.ds(row, 48), pl.ds(pl.multiple_of(core * HALF, 128), HALF)],
                        wo_sem.at[i * 4 + j],
                    )
                )
    for copy in copies + late:
        copy.start()
    return copies, late


def wait_all(copies):
    for copy in copies:
        copy.wait()


def project(normed, weights, projected):
    projected[...] = jnp.dot(normed[...], weights[...], preferred_element_type=F32).astype(BF16)


def start_all(pairs, sems):
    copies = [
        pltpu.make_async_copy(source, target, sems.at[i]) for i, (source, target) in enumerate(pairs)
    ]
    for copy in copies:
        copy.start()
    return copies


def attend(projected, store):
    rows = projected.shape[0]
    block = 256
    low = lax.broadcasted_iota(jnp.int32, (block, 128), 1) < 64
    for pair in range(3):
        at = pair * 128
        k = projected[:, HALF + at : HALF + at + 128]
        v = projected[:, 2 * HALF + at : 2 * HALF + at + 128]
        values = jnp.concatenate([v, jnp.ones((rows, 128), BF16)], axis=1)
        for row in range(0, rows, block):
            q = projected[row : row + block, at : at + 128] * jnp.asarray(0.125, BF16)
            zero = jnp.zeros_like(q)
            outs = []
            for side in range(2):
                mine = jnp.where(low, q, zero) if side == 0 else jnp.where(low, zero, q)
                scores = lax.dot_general(
                    mine, k, (((1,), (1,)), ((), ())), preferred_element_type=F32
                )
                weight = jnp.exp(scores - jnp.max(scores, -1, keepdims=True)).astype(BF16)
                total = jnp.dot(weight, values, preferred_element_type=F32)
                outs.append(total[:, :128] / total[:, 128:])
            store(pair, row, jnp.where(low, outs[0], outs[1]).astype(BF16))


def prepare_kernel(x_ref, gain_ref, row_ref, normed_ref, position_ref):
    rows = x_ref.shape[1]
    normed_ref[0] = scale_rows(x_ref[0], gain_ref[...]).astype(BF16)
    ids_row = row_ref[0]
    i0 = lax.broadcasted_iota(jnp.int32, (rows, rows), 0)
    i1 = lax.broadcasted_iota(jnp.int32, (rows, rows), 1)
    picked = ids_row == lax.broadcasted_iota(jnp.int32, (EXPERTS, rows), 0)
    running = jnp.dot(
        picked.astype(F32).astype(BF16),
        (i0 <= i1).astype(F32).astype(BF16),
        preferred_element_type=F32,
    )
    rank = jnp.sum(jnp.where(picked, running, 0.0), 0, keepdims=True)
    position_ref[0] = ids_row * SLOTS + rank.astype(jnp.int32) - 1


def context_kernel(n_ref, b0, b1, ctx_ref, normed, w, projected, sem, small):
    core = my_core()
    loads = start_all([(n_ref.at[0], normed)], small)
    copies, _ = fetch((b0, b1), core, w, sem)
    wait_all(loads + copies)
    project(normed, w.at[core], projected)

    def store(pair, row, context):
        ctx_ref[row : row + context.shape[0], pair * 128 : pair * 128 + 128] = context

    attend(projected, store)


def finish(
    x, ctx, wo, gain, router, ids, place_row, att_ref, out_ref, aux_ref, normed, sent, att, aux, sems
):
    rows, experts = x.shape[0], router.shape[1]
    block = 256
    for row in range(0, rows, block):
        mine = slice(row, row + block)
        both = jnp.concatenate([ctx[0, mine], ctx[1, mine]], axis=1)
        mixed = jnp.dot(both, wo[...], preferred_element_type=F32)
        attended = (x[mine].astype(F32) + mixed).astype(BF16)
        att[mine] = attended
        normed[mine] = scale_rows(attended, gain[...]).astype(BF16)
    copies = [pltpu.make_async_copy(att, att_ref, sems.at[4])]
    copies[0].start()
    position = place_row[...]
    for slot in range(0, experts * SLOTS, block):
        number = lax.broadcasted_iota(jnp.int32, (block, rows), 0) + slot
        spread = (number == position).astype(F32).astype(BF16)
        some = pl.ds(slot // SLOTS, block // SLOTS)
        sent[some] = (
            jnp.dot(spread, normed[...], preferred_element_type=F32)
            .astype(BF16)
            .reshape(block // SLOTS, SLOTS, normed.shape[1])
        )
        copy = pltpu.make_async_copy(sent.at[some], out_ref.at[some], sems.at[slot // block])
        copy.start()
        copies.append(copy)
    ids_row = ids[...]
    logits = lax.dot_general(
        router[...], normed[...], (((0,), (1,)), ((), ())), preferred_element_type=F32
    )
    picked = ids_row == lax.broadcasted_iota(jnp.int32, (experts, rows), 0)
    gate = jax.nn.sigmoid(jnp.sum(jnp.where(picked, logits, 0.0), 0, keepdims=True))
    aux_row = lax.broadcasted_iota(jnp.int32, (128, rows), 0)
    aux[...] = jnp.where(aux_row == 0, gate, position.astype(F32)).T
    copies.append(pltpu.make_async_copy(aux, aux_ref, sems.at[5]))
    copies[-1].start()
    wait_all(copies)


def second_half_kernel(
    x_ref, n_ref, m0, m1, o0, o1, ctx_ref, gain_ref, router_ref, row_ref, position_ref,
    att_ref, out_ref, aux_ref,
    x, gain, router, ids, place_row, w, wo, ctx, projected, normed, sent, att, aux, sems, small,
):
    core = my_core()
    qkv, late = fetch((o0, o1), 1 - core, w, sems.at[0], wo, sems.at[1])
    _, later = fetch((m0, m1), core, None, None, wo, sems.at[2])
    loads = start_all(
        [
            (x_ref.at[0], x), (gain_ref, gain), (router_ref, router), (row_ref.at[0], ids),
            (position_ref.at[0], place_row),
        ],
        small,
    )
    ctx[core] = ctx_ref[...]
    wait_all(qkv)
    project(n_ref, w.at[1 - core], projected)

    def store(pair, row, context):
        ctx[1 - core, row : row + context.shape[0], pair * 128 : pair * 128 + 128] = context

    attend(projected, store)
    wait_all(late + later + loads)
    finish(
        x, ctx, wo, gain, router, ids, place_row, att_ref, out_ref, aux_ref,
        normed, sent, att, aux, small,
    )


def whole_kernel(
    x_ref, n_ref, m0, m1, o0, o1, gain_ref, router_ref, row_ref, position_ref,
    att_ref, out_ref, aux_ref,
    x, gain, router, ids, place_row, w, wo, ctx, projected, normed, sent, att, aux, sems, small,
):
    core = my_core()
    first = start_all([(n_ref.at[1], normed)], small.at[pl.ds(5, 1)])
    qkv, late = fetch((m0, m1), core, w, sems.at[0], wo, sems.at[1])
    qkv2, late2 = fetch((o0, o1), 1 - core, w, sems.at[2], wo, sems.at[3])
    loads = start_all(
        [
            (x_ref.at[1], x), (gain_ref, gain), (router_ref, router), (row_ref.at[1], ids),
            (position_ref.at[1], place_row),
        ],
        small,
    )
    wait_all(first + qkv + qkv2)

    def step(side, carry):
        def store(pair, row, context):
            ctx[side, row : row + context.shape[0], pair * 128 : pair * 128 + 128] = context

        project(normed, w.at[side], projected)
        attend(projected, store)
        return carry

    lax.fori_loop(0, 2, step, 0)
    wait_all(late + late2 + loads)
    finish(
        x, ctx, wo, gain, router, ids, place_row, att_ref, out_ref, aux_ref,
        normed, sent, att, aux, small,
    )


def expert_kernel(x_ref, in_ref, out_ref, y_ref, total, hidden):
    step = pl.program_id(0)
    slots, width = total.shape
    block = 256
    x = x_ref.reshape(slots, width)

    @pl.when(step == 0)
    def _():
        total[...] = jnp.zeros_like(total)

    for at in range(0, slots, block):
        first = jnp.dot(x[at : at + block], in_ref[0], preferred_element_type=F32)
        hidden[at : at + block] = jnp.maximum(first, 0.0).astype(BF16)
    for at in range(0, slots, block):
        total[at : at + block] += jnp.dot(
            hidden[at : at + block], out_ref[0], preferred_element_type=F32
        )

    @pl.when(step == pl.num_programs(0) - 1)
    def _():
        y_ref[...] = total[...].astype(BF16).reshape(y_ref.shape)


def combine_kernel(batch, att_ref, aux_ref, back_ref, out_ref, att, aux, done, sems):
    rows, width = att.shape
    slots = back_ref.shape[0] * SLOTS
    block = 128
    back = back_ref.reshape(slots, width)
    loads = start_all([(aux_ref, aux), (att_ref, att)], sems.at[pl.ds(4, 2)])
    loads[0].wait()
    copies = []
    for row in range(0, rows, block):
        mine = pl.ds(row, block)
        gate = aux[mine, 0:1]
        position = aux[mine, 1:2].astype(jnp.int32)
        pick = lax.broadcasted_iota(jnp.int32, (block, slots), 1) == position
        result = jnp.dot(pick.astype(F32).astype(BF16), back[...], preferred_element_type=F32)
        if row == 0:
            loads[1].wait()
        done[mine] = (att[mine].astype(F32) + gate * result).astype(BF16)
        copy = pltpu.make_async_copy(done.at[mine], out_ref.at[batch, mine], sems.at[row // block])
        copy.start()
        copies.append(copy)
    wait_all(copies)


def combine_after_kernel(batch, att_ref, aux_ref, back_ref, held_ref, out_ref, *scratch):
    del held_ref
    combine_kernel(batch, att_ref, aux_ref, back_ref, out_ref, *scratch)


def limit(kibibytes):
    return pltpu.CompilerParams(vmem_limit_bytes=kibibytes << 10)


def full(shape):
    return pl.BlockSpec(shape, lambda i: (0,) * len(shape))


def body(
    tokens, expert_ids, attn_qkv, attn_out, norm_attn, norm_ffn, router, expert_in, expert_out
):
    batches, rows, width = tokens.shape
    experts = router.shape[1]
    slots = experts * SLOTS
    core = my_core()
    halves = [
        jnp.concatenate(
            [attn_qkv[:, at + side * HALF : at + side * HALF + HALF] for at in (0, width, 2 * width)]
            + [attn_out[:, side * HALF : side * HALF + HALF]],
            axis=1,
        )
        for side in range(2)
    ]
    piece = jnp.where(core == 0, halves[0], halves[1])
    swap = [(i, i ^ 1) for i in range(128)]
    steps = (1, -1, 2)
    own = jnp.concatenate([piece] + [lax.ppermute(piece, ALL, hop(d, 0)) for d in steps], axis=0)
    ids_row = expert_ids.reshape(batches, 1, rows)
    normed, position = pl.pallas_call(
        prepare_kernel,
        grid=(batches,),
        out_shape=(
            jax.ShapeDtypeStruct((batches, rows, width), BF16),
            jax.ShapeDtypeStruct((batches, 1, rows), jnp.int32),
        ),
        in_specs=[
            pl.BlockSpec((1, rows, width), lambda b: (b, 0, 0)),
            pl.BlockSpec((width,), lambda b: (0,)),
            pl.BlockSpec((1, 1, rows), lambda b: (b, 0, 0)),
        ],
        out_specs=(
            pl.BlockSpec((1, rows, width), lambda b: (b, 0, 0)),
            pl.BlockSpec((1, 1, rows), lambda b: (b, 0, 0)),
        ),
        compiler_params=limit(47104),
        name="prepare",
    )(tokens, norm_attn, ids_row)
    own, normed, position = lax.optimization_barrier((own, normed, position))
    rest = jnp.concatenate([lax.ppermute(own, ALL, hop(d, 1)) for d in steps], axis=0)
    mine = [own, rest]
    other = [lax.ppermute(part, ALL, swap) for part in mine]
    mine = [pltpu.with_memory_space_constraint(part, pltpu.VMEM) for part in mine]
    other = [pltpu.with_memory_space_constraint(part, pltpu.VMEM) for part in other]

    any_spec = pl.BlockSpec(memory_space=pltpu.HBM)
    whole = pl.BlockSpec(memory_space=pltpu.VMEM)

    def near(value):
        return pltpu.with_memory_space_constraint(value, pltpu.VMEM)

    def far(value):
        return pltpu.with_memory_space_constraint(value, pltpu.HBM)

    w_scratch = pltpu.VMEM((2, width, 3 * HALF), BF16)
    projected = pltpu.VMEM((rows, 3 * HALF), BF16)
    one = pltpu.VMEM((rows, width), BF16)
    gain_scratch = pltpu.VMEM((width,), F32)
    ctx_mine, normed_first = pl.pallas_call(
        context_kernel,
        out_shape=(
            jax.ShapeDtypeStruct((rows, HALF), BF16),
            jax.ShapeDtypeStruct((rows, width), BF16),
        ),
        in_specs=[any_spec] + [whole] * 2,
        out_specs=(whole, whole),
        scratch_shapes=[
            w_scratch,
            projected,
            pltpu.SemaphoreType.DMA((16,)),
            pltpu.SemaphoreType.DMA((1,)),
        ],
        compiler_params=limit(47104),
        name="first_half",
    )(normed, *mine)

    finish_out = (
        jax.ShapeDtypeStruct((rows, width), BF16),
        jax.ShapeDtypeStruct((experts, SLOTS, width), BF16),
        jax.ShapeDtypeStruct((rows, 128), F32),
    )
    finish_specs = (any_spec, any_spec, any_spec)
    scratch = [
        one,
        gain_scratch,
        pltpu.VMEM((width, experts), BF16),
        pltpu.VMEM((1, rows), jnp.int32),
        pltpu.VMEM((1, rows), jnp.int32),
        w_scratch,
        pltpu.VMEM((width, width), BF16),
        pltpu.VMEM((2, rows, HALF), BF16),
        projected,
        one,
        pltpu.VMEM((experts, SLOTS, width), BF16),
        one,
        pltpu.VMEM((rows, 128), F32),
        pltpu.SemaphoreType.DMA((4, 16)),
        pltpu.SemaphoreType.DMA((6,)),
    ]

    first = pl.pallas_call(
        second_half_kernel,
        out_shape=finish_out,
        in_specs=[any_spec] + [whole] * 6 + [any_spec] * 4,
        out_specs=finish_specs,
        scratch_shapes=scratch,
        compiler_params=limit(54000),
        name="second_half",
    )(tokens, near(normed_first), *mine, *other, near(ctx_mine), norm_ffn, router, ids_row, position)

    second = pl.pallas_call(
        whole_kernel,
        out_shape=finish_out,
        in_specs=[any_spec] * 2 + [whole] * 4 + [any_spec] * 4,
        out_specs=finish_specs,
        scratch_shapes=scratch,
        compiler_params=limit(54000),
        name="whole",
    )(tokens, normed, *mine, *other, norm_ffn, router, ids_row, position)

    def exchange(values):
        moved = lax.all_to_all(values, ALL, split_axis=0, concat_axis=0, tiled=True)
        return pltpu.with_memory_space_constraint(moved, pltpu.VMEM)

    hidden = expert_in.shape[2]
    chunk = 512
    def serve(values):
        return pl.pallas_call(
            expert_kernel,
            grid=(hidden // chunk,),
            out_shape=jax.ShapeDtypeStruct((experts, SLOTS, width), BF16),
            in_specs=[
                whole,
                pl.BlockSpec((1, width, chunk), lambda j: (0, 0, j)),
                pl.BlockSpec((1, chunk, width), lambda j: (0, j, 0)),
            ],
            out_specs=pl.BlockSpec((experts, SLOTS, width), lambda j: (0, 0, 0)),
            scratch_shapes=[pltpu.VMEM((slots, width), F32), pltpu.VMEM((slots, chunk), BF16)],
            compiler_params=limit(58300),
            name="expert",
        )(values, far(expert_in), far(expert_out))

    arrived = [exchange(first[1]), exchange(second[1])]
    back = [exchange(serve(values)) for values in arrived]

    out_shape = jax.ShapeDtypeStruct((batches, rows, width), BF16)
    combine_scratch = [
        one,
        pltpu.VMEM((rows, 128), F32),
        one,
        pltpu.SemaphoreType.DMA((6,)),
    ]
    held = pl.pallas_call(
        functools.partial(combine_kernel, 0),
        out_shape=out_shape,
        in_specs=[any_spec] * 2 + [whole],
        out_specs=any_spec,
        scratch_shapes=combine_scratch,
        compiler_params=limit(58300),
        name="combine0",
    )(first[0], first[2], back[0])
    return pl.pallas_call(
        functools.partial(combine_after_kernel, 1),
        out_shape=out_shape,
        in_specs=[any_spec] * 2 + [whole, any_spec],
        out_specs=any_spec,
        scratch_shapes=combine_scratch,
        input_output_aliases={3: 0},
        compiler_params=limit(58300),
        name="combine1",
    )(second[0], second[2], back[1], held)


def solution(mesh):
    in_specs = (
        P(None, ALL, None),
        P(None, ALL, None),
        P(("seq", "role"), None),
        P(("seq", "role"), None),
        P(),
        P(),
        P(),
        P(ALL, None, None),
        P(ALL, None, None),
    )
    return jax.shard_map(
        body, mesh=mesh, in_specs=in_specs, out_specs=P(None, ALL, None), check_vma=False
    )
```
